32 devices in a mesh: seq: 8 (over z, x), head: 4 (over y, core).
Axes of the slice: x: 2, y: 2, z: 4, core: 2. Of those that a mesh axis runs over, the one named last changes fastest.
Arguments:
- tokens_in: bfloat16 [256, 32, 6144], P('seq', None, 'head'), may hold values from -6 to 6
- gate_rows: bfloat16 [256, 32, 6144], P('seq', None, 'head'), may hold values from -28 to 28
- gate_cols: bfloat16 [256, 32, 6144], P(None, 'seq', 'head'), may hold values from -28 to 28
- write_rows: bfloat16 [64, 8192], P(None, 'seq'), may hold values from -6 to 6
- read_rows: bfloat16 [64, 8192], P(None, 'seq'), may hold values from -0.75 to 0.75
- step_rows: float32 [48, 8192], P('head', 'seq'), may hold values from 0 to 2, as said below
- decay_rows: float32 [48, 8192], P('head', 'seq'), may hold values from -1 to 0, as said below
- skip_rows: float32 [48], P('head'), may hold values from 0.5 to 2
- norm_rows: float32 [6144], P('head'), may hold values from 0.5 to 1.5
- write_cols: bfloat16 [64, 8192], P(None, 'seq'), may hold values from -6 to 6
- read_cols: bfloat16 [64, 8192], P(None, 'seq'), may hold values from -0.75 to 0.75
- step_cols: float32 [48, 8192], P('head', 'seq'), may hold values from 0 to 2, as said below
- decay_cols: float32 [48, 8192], P('head', 'seq'), may hold values from -1 to 0, as said below
- skip_cols: float32 [48], P('head'), may hold values from 0.5 to 2
- norm_cols: float32 [6144], P('head'), may hold values from 0.5 to 1.5
Outputs:
- mixed_cols: bfloat16 [256, 32, 6144], P(None, 'seq', 'head')
The draws below stay inside these ranges and needn't reach their ends.
Inputs may be any that keep to these rules, and one draw needn't show every extreme that they name: `step_rows`: positive. `step_cols`: positive. `decay_rows`: never positive. `decay_cols`: never positive.
All inputs are finite; a program needn't handle non-finite values.
Results may differ from the reference program's by a relative error of at most 0.0063.
Values may be sent and summed in bfloat16 or wider, within the bound.
A program may use at most 128 MiB of HBM per device.

```python
import math
import jax
import jax.numpy as jnp
from jax import lax

HEADS = 48
HEADDIM = 128
NSTATE = 64
BLOCK = 256
GRID_W = 32
ROWS = 256
LENGTH = 8192
INNER = 6144


def head_laws(key, salt):
    folded = jax.random.fold_in(key, salt)
    keys = jax.random.split(folded, 7)
    share = 0.5
    slow_heads = jax.random.uniform(keys[0], (HEADS,)) < share
    slow_rate = jax.random.uniform(keys[1], (HEADS,), minval=0.05, maxval=0.5) / LENGTH
    fast_rate = jax.random.uniform(keys[2], (HEADS,), minval=1.0 / 50.0, maxval=1.0 / 30.0)
    each_head_values = jnp.where(slow_heads, slow_rate, fast_rate)
    coarse_estimate = jax.random.uniform(keys[3], (HEADS, LENGTH), minval=0.5, maxval=1.5)
    spread = jax.random.uniform(keys[6], (HEADS, LENGTH), minval=0.5, maxval=1.5)
    grid_points = jax.random.randint(keys[4], (2,), 0, LENGTH)
    retained_values = jax.random.uniform(keys[5], (2,), minval=0.5, maxval=0.8)
    token_locations = jnp.arange(LENGTH, dtype=jnp.int32)
    sudden_jump = jnp.sum(jnp.where(token_locations[None, :] == grid_points[:, None], jnp.log(retained_values)[:, None], 0.0), axis=0)
    decay_factors = -each_head_values[:, None] * coarse_estimate + sudden_jump[None, :]
    scales = jnp.where(slow_heads, jnp.sqrt(40.0 / LENGTH), 1.0)
    steps = scales[:, None] * spread
    return (steps.astype(jnp.float32), decay_factors.astype(jnp.float32))


def gate_draw(key, salt):
    folded = jax.random.fold_in(key, salt)
    head_index = jnp.arange(INNER, dtype=jnp.int32) // HEADDIM
    fraction = head_index.astype(jnp.float32) / (HEADS - 1)
    scales = 4.0 ** fraction
    values = jnp.clip(jax.random.normal(folded, (ROWS, GRID_W, INNER)), -3.0, 3.0)
    return (values * scales).astype(jnp.bfloat16)


def draw_gate_rows(key, part):
    return gate_draw(key, 31)


def draw_gate_cols(key, part):
    return gate_draw(key, 37)


def draw_step_rows(key, part):
    return head_laws(key, 11)[0]


def draw_decay_rows(key, part):
    return head_laws(key, 11)[1]


def draw_step_cols(key, part):
    return head_laws(key, 23)[0]


def draw_decay_cols(key, part):
    return head_laws(key, 23)[1]


def steps_of(own_key, dims, cuts, smallest, high):
    gain = 1.0
    for axis_at, blocks in cuts:
        draws = jax.random.uniform(jax.random.fold_in(jax.random.fold_in(own_key, 6), axis_at), (blocks,), jnp.float32, smallest / len(cuts), high / len(cuts))
        gain = gain * jnp.repeat(jnp.exp(draws), dims[axis_at] // blocks).reshape((-1,) + (1,) * (len(dims) - 1 - axis_at))
    return gain


def centred(rng, extent, scale, limit, cuts=(), kind=jnp.bfloat16):
    array = jax.random.normal(rng, extent, jnp.float32) * scale
    if len(cuts) > 0:
        array = steps_of(rng, extent, cuts, -0.22, 0.18) * array
    return jnp.clip(array, min=-limit, max=limit).astype(kind)


def setup_inputs(seed: int = 0) -> dict:
    arg_keys = jax.random.split(jax.random.key(seed), 16)
    tokens_in = centred(arg_keys[0], (ROWS, GRID_W, INNER), 1.0, 6.0, ((0, 8), (2, 4)))
    gate_rows = draw_gate_rows(jax.random.fold_in(arg_keys[15], 71), 0)
    gate_cols = draw_gate_cols(jax.random.fold_in(arg_keys[15], 71), 0)
    write_rows = centred(arg_keys[3], (NSTATE, LENGTH), 1.0, 6.0, ((1, 8),))
    read_rows = centred(arg_keys[4], (NSTATE, LENGTH), NSTATE ** -0.5, 0.75, ((1, 8),))
    step_rows = draw_step_rows(jax.random.fold_in(arg_keys[15], 71), 0)
    decay_rows = draw_decay_rows(jax.random.fold_in(arg_keys[15], 71), 0)
    skip_rows = jnp.clip(jnp.exp(math.log(2.0) - 1.3862944 * jax.random.uniform(arg_keys[7], (HEADS,), jnp.float32) ** steps_of(arg_keys[7], (HEADS,), ((0, 4),), -0.2, 0.2)), 0.5, 2.0)
    norm_rows = jnp.clip(1.0 + 0.1 * jax.random.normal(arg_keys[8], (INNER,), jnp.float32), 0.5, 1.5)
    write_cols = centred(arg_keys[9], (NSTATE, LENGTH), 1.0, 6.0, ((1, 8),))
    read_cols = centred(arg_keys[10], (NSTATE, LENGTH), NSTATE ** -0.5, 0.75, ((1, 8),))
    step_cols = draw_step_cols(jax.random.fold_in(arg_keys[15], 71), 0)
    decay_cols = draw_decay_cols(jax.random.fold_in(arg_keys[15], 71), 0)
    skip_cols = jnp.clip(jnp.exp(math.log(2.0) - 1.3862944 * jax.random.uniform(arg_keys[13], (HEADS,), jnp.float32) ** steps_of(arg_keys[13], (HEADS,), ((0, 4),), -0.2, 0.2)), 0.5, 2.0)
    norm_cols = jnp.clip(1.0 + 0.1 * jax.random.normal(arg_keys[14], (INNER,), jnp.float32), 0.5, 1.5)
    return dict(tokens_in=tokens_in, gate_rows=gate_rows, gate_cols=gate_cols, write_rows=write_rows, read_rows=read_rows, step_rows=step_rows, decay_rows=decay_rows, skip_rows=skip_rows, norm_rows=norm_rows, write_cols=write_cols, read_cols=read_cols, step_cols=step_cols, decay_cols=decay_cols, skip_cols=skip_cols, norm_cols=norm_cols)


EPSILON = 1e-05
HIGHEST = lax.Precision.HIGHEST

def block_step(state_in, inputs, gate_blk, write_blk, read_blk, step_blk, decay_blk, skip_vec, gain_vec):
    length = inputs.shape[0]
    causal = lax.broadcasted_iota(jnp.int32, (length, length), 0) >= lax.broadcasted_iota(jnp.int32, (length, length), 1)
    cumulative = jnp.cumsum(decay_blk, axis=1)
    scores = jnp.dot(read_blk.T, write_blk, preferred_element_type=jnp.float32)
    spread = cumulative[:, :, None] - cumulative[:, None, :]
    fading = jnp.where(causal, jnp.exp(jnp.where(causal, spread, 0.0)), 0.0)
    mixing = (fading * scores[None] * step_blk[:, None, :]).astype(jnp.bfloat16)
    wide_in = inputs.astype(jnp.float32)
    inner_part = jnp.einsum('hts,shp->thp', mixing.astype(jnp.float32), wide_in)
    tail_weights = jnp.exp(cumulative[:, -1:] - cumulative) * step_blk
    loaded = (write_blk.astype(jnp.float32)[None] * tail_weights[:, None, :]).astype(jnp.bfloat16)
    gained = jnp.einsum('hns,shp->hnp', loaded.astype(jnp.float32), wide_in)
    from_state = jnp.einsum('nt,hnp->thp', read_blk.astype(jnp.float32), state_in, precision=HIGHEST)
    outputs = inner_part + from_state * jnp.exp(cumulative).T[:, :, None] + skip_vec[:, None] * wide_in
    gated = outputs.reshape(length, -1) * jax.nn.silu(gate_blk.astype(jnp.float32))
    scaled = lax.rsqrt(lax.optimization_barrier(jnp.mean(gated * gated, axis=-1)) + EPSILON)
    result = (gated * scaled[:, None] * gain_vec).astype(jnp.bfloat16)
    new_state = jnp.exp(cumulative[:, -1])[:, None, None] * state_in + gained
    return (new_state, result)

def run_layer(fetch, block_total, write_mat, read_mat, step_mat, decay_mat, skip_vec, gain_vec):
    head_count = step_mat.shape[0]
    state_size = write_mat.shape[0]
    head_width = gain_vec.shape[0] // head_count

    def window_of(matrix, offset):
        return lax.dynamic_slice_in_dim(matrix, offset, BLOCK, 1)

    def advance(state_in, block_index):
        inputs, gate_blk = fetch(block_index)
        offset = (block_index * BLOCK).astype(jnp.int32)
        return block_step(state_in, inputs, gate_blk, window_of(write_mat, offset), window_of(read_mat, offset), window_of(step_mat, offset), window_of(decay_mat, offset), skip_vec, gain_vec)
    initial = jnp.zeros((head_count, state_size, head_width), jnp.float32)
    return lax.scan(advance, initial, jnp.arange(block_total, dtype=jnp.int32))[1]

def reference(tokens_in, gate_rows, gate_cols, write_rows, read_rows, step_rows, decay_rows, skip_rows, norm_rows, write_cols, read_cols, step_cols, decay_cols, skip_cols, norm_cols):
    flat_tokens = tokens_in.reshape(LENGTH, INNER)
    flat_gate = gate_rows.reshape(LENGTH, INNER)

    def fetch_rows(block_index):
        offset = (block_index * BLOCK).astype(jnp.int32)
        token_block = lax.dynamic_slice_in_dim(flat_tokens, offset, BLOCK, 0).reshape(BLOCK, HEADS, HEADDIM)
        return (token_block, lax.dynamic_slice_in_dim(flat_gate, offset, BLOCK, 0))
    first = run_layer(fetch_rows, LENGTH // BLOCK, write_rows, read_rows, step_rows, decay_rows, skip_rows, norm_rows)
    hidden = first.reshape(ROWS, GRID_W, INNER)
    per_col = ROWS // BLOCK

    def fetch_cols(block_index):
        column = (block_index // per_col).astype(jnp.int32)
        row_start = (block_index % per_col * BLOCK).astype(jnp.int32)
        zero_index = jnp.zeros((), jnp.int32)
        token_block = lax.dynamic_slice(hidden, (row_start, column, zero_index), (BLOCK, 1, INNER)).reshape(BLOCK, HEADS, HEADDIM)
        gate_block = lax.dynamic_slice(gate_cols, (row_start, column, zero_index), (BLOCK, 1, INNER)).reshape(BLOCK, INNER)
        return (token_block, gate_block)
    second = run_layer(fetch_cols, LENGTH // BLOCK, write_cols, read_cols, step_cols, decay_cols, skip_cols, norm_cols)
    return second.reshape(GRID_W, per_col, BLOCK, INNER).transpose(1, 2, 0, 3).reshape(ROWS, GRID_W, INNER)
```

```python
import functools
import jax
import jax.numpy as jnp
from jax import lax
from jax.experimental import pallas as pl
from jax.experimental.pallas import tpu as pltpu
from jax.sharding import PartitionSpec as P

BLOCK = 256
LANES = 128
EPSILON = 1e-05
LOG2E = 1.4426950408889634
HIGHEST = lax.Precision.HIGHEST
MESH = pl.DeviceIdType.MESH
F32 = jnp.float32
BF16 = jnp.bfloat16
VMEM_BYTES = 60 * 1024 * 1024


def contract(a, b, dims, precision=None):
    return lax.dot_general(
        a, b, (dims, ((), ())), precision=precision, preferred_element_type=F32
    )


def iota(shape, axis):
    return lax.broadcasted_iota(jnp.int32, shape, axis)


def block_sums(decay):
    upper = (iota((BLOCK, BLOCK), 0) <= iota((BLOCK, BLOCK), 1)).astype(F32)
    cumulative = contract(decay, upper, ((1,), (0,)), HIGHEST)
    total = contract(decay, jnp.ones((BLOCK, LANES), F32), ((1,), (0,)), HIGHEST)
    return cumulative, total


def head_state(write32, weight_row, tokens):
    loaded = (write32 * weight_row).astype(BF16)
    return contract(loaded, tokens, ((1,), (0,)))


def states_kernel(heads, x_ref, write_ref, step_ref, decay_ref, end_ref, total_ref):
    step_at = pl.program_id(0)

    @pl.when(step_at == 0)
    def _():
        end_ref[...] = jnp.zeros_like(end_ref)
        total_ref[...] = jnp.zeros_like(total_ref)

    cumulative, total = block_sums(decay_ref[...] * LOG2E)
    tokens = x_ref[...].reshape(BLOCK, x_ref.shape[-1])
    write32 = write_ref[...].astype(F32)
    final = total[:, :1]
    weights = jnp.exp2(final - cumulative) * step_ref[...]
    fade = jnp.exp2(total)
    for h in range(heads):
        gained = head_state(write32, weights[h : h + 1], tokens[:, h * LANES : (h + 1) * LANES])
        end_ref[h] = fade[h : h + 1] * end_ref[h] + gained
    total_ref[...] += total


def main_kernel(
    heads, skip_ref, x_ref, gate_ref, write_ref, read_ref, step_ref, decay_ref, prior_ref,
    gated_ref, squares_ref, state,
):
    @pl.when(pl.program_id(0) == 0)
    def _():
        state[...] = prior_ref[...].astype(F32)

    decay = decay_ref[...] * LOG2E
    step = step_ref[...]
    cumulative, total = block_sums(decay)
    lower = (iota((BLOCK, BLOCK), 0) >= iota((BLOCK, BLOCK), 1)).astype(F32)
    across = contract(lower, decay, ((1,), (1,)), HIGHEST)
    lifting = jnp.exp2(across)
    tokens = x_ref[...].reshape(BLOCK, x_ref.shape[-1])
    write = write_ref[...]
    read = read_ref[...]
    write32 = write.astype(F32)
    scores = contract(read, write, ((0,), (0,))) * lower
    weights = jnp.exp2(total[:, :1] - cumulative) * step
    fade = jnp.exp2(total)
    squares = jnp.zeros((BLOCK, LANES), F32)
    for h in range(heads):
        lanes = slice(h * LANES, (h + 1) * LANES)
        own = tokens[:, lanes]
        spread = jnp.minimum(across[:, h : h + 1] - cumulative[h : h + 1], 0.0)
        mixing = (jnp.exp2(spread) * scores * step[h : h + 1]).astype(BF16)
        held = state[h]
        out = contract(mixing, own, ((1,), (0,)))
        out += lifting[:, h : h + 1] * contract(read, held.astype(BF16), ((0,), (0,)))
        out += skip_ref[h] * own.astype(F32)
        gate = gate_ref[0, :, lanes].astype(F32)
        gated = out * (gate / (1.0 + jnp.exp2(gate * -LOG2E)))
        squares += gated * gated
        gated_ref[0, :, lanes] = gated.astype(BF16)
        state[h] = fade[h : h + 1] * held + head_state(write32, weights[h : h + 1], own)
    squares_ref[0] = contract(jnp.ones((8, LANES), F32), squares, ((1,), (1,)), HIGHEST)


def norm_kernel(inner, cols, gated_ref, squares_ref, gain_ref, out_ref):
    high = BLOCK // cols
    to = iota((BLOCK, BLOCK), 0)
    source = (to % high) * cols + to // high
    chosen = source == iota((BLOCK, BLOCK), 1)
    sums = contract(chosen.astype(F32), squares_ref[0], ((1,), (1,)), HIGHEST)
    scaled = lax.rsqrt(sums[:, :1] / inner + EPSILON)
    if cols > 1:
        gated = contract(chosen.astype(BF16), gated_ref[0], ((1,), (0,)))
    else:
        gated = gated_ref[0].astype(F32)
    result = gated * scaled * gain_ref[...]
    out_ref[...] = result.reshape(out_ref.shape).astype(BF16)


def greet(axis, count):
    me = lax.axis_index(axis)
    barrier = pltpu.get_barrier_semaphore()
    for hop in range(1, count):
        pl.semaphore_signal(
            barrier, inc=1, device_id={axis: lax.rem(me + hop, count)}, device_id_type=MESH
        )
    pl.semaphore_wait(barrier, count - 1)
    return me


def sum_kernel(count, own_ref, out_ref, held, send_sems, recv_sems):
    me = greet("head", count)
    copies = []
    for hop in range(1, count):
        copy = pltpu.make_async_remote_copy(
            src_ref=own_ref,
            dst_ref=held.at[hop - 1],
            send_sem=send_sems.at[hop - 1],
            recv_sem=recv_sems.at[hop - 1],
            device_id={"head": lax.rem(me + hop, count)},
            device_id_type=MESH,
        )
        copy.start()
        copies.append(copy)
    for copy in copies:
        copy.wait()
    total = own_ref[...]
    for hop in range(1, count):
        total += held[hop - 1]
    out_ref[...] = total


def trade_kernel(count, own_ref, out_ref, send_sems, recv_sems, local_sem):
    me = greet("seq", count)
    copies = []
    for hop in range(count // 2, count // 2 + count - 1):
        ahead = 1 + (hop - 1) % (count - 1)
        to = lax.rem(me + ahead, count)
        copy = pltpu.make_async_remote_copy(
            src_ref=own_ref.at[to],
            dst_ref=out_ref.at[me],
            send_sem=send_sems.at[ahead - 1],
            recv_sem=recv_sems.at[ahead - 1],
            device_id={"seq": to},
            device_id_type=MESH,
        )
        copy.start()
        copies.append(copy)
    local = pltpu.make_async_copy(own_ref.at[me], out_ref.at[me], local_sem)
    local.start()
    local.wait()
    for copy in copies:
        copy.wait()


def prior_kernel(
    count, end_ref, total_ref, prior_ref, totals, sent, swapped, pair, pairs, back, start, landed,
    total_send, total_recv, swap_sems, pair_send, pair_recv, back_sems,
):
    heads = end_ref.shape[0]
    half = heads // 2
    me = greet("seq", count)
    place = lax.rem(me, 2)
    partner = me + 1 - 2 * place
    group = me // 2
    groups = count // 2
    keep = place * half
    give = half - keep

    sent[...] = end_ref[pl.ds(give, half)].astype(BF16)
    swap = pltpu.make_async_remote_copy(
        src_ref=sent, dst_ref=swapped, send_sem=swap_sems.at[0], recv_sem=swap_sems.at[1],
        device_id={"seq": partner}, device_id_type=MESH,
    )
    swap.start()
    total_copies = []
    for hop in range(1, count):
        copy = pltpu.make_async_remote_copy(
            src_ref=total_ref, dst_ref=totals.at[hop], send_sem=total_send.at[hop - 1],
            recv_sem=total_recv.at[hop - 1],
            device_id={"seq": lax.rem(me + hop, count)}, device_id_type=MESH,
        )
        copy.start()
        total_copies.append(copy)
    totals[0] = total_ref[...]
    for copy in total_copies:
        copy.wait()
    swap.wait()

    def total_of(device):
        return totals[lax.rem(me - device + count, count)]

    odd = place.astype(F32)
    even_total = total_of(group * 2)
    odd_total = total_of(group * 2 + 1)
    odd_fade = jnp.exp2(odd_total)
    even_fade = jnp.exp2(even_total)
    for h in range(half):
        mine = end_ref[keep + h]
        other = swapped[h].astype(F32)
        first = odd * other + (1.0 - odd) * mine
        last = odd * mine + (1.0 - odd) * other
        row = jnp.where(place == 0, odd_fade[h : h + 1], odd_fade[half + h : half + h + 1])
        pair[h] = (row * first + last).astype(BF16)
        start[h] = first

    def pair_copy(hop):
        return pltpu.make_async_remote_copy(
            src_ref=pair, dst_ref=pairs.at[hop - 1], send_sem=pair_send.at[hop - 1],
            recv_sem=pair_recv.at[hop - 1],
            device_id={"seq": lax.rem(me + 2 * hop, count)}, device_id_type=MESH,
        )

    for hop in range(1, groups):

        @pl.when(group + hop < groups)
        def _():
            pair_copy(hop).start()

    for h in range(half):
        row = jnp.where(place == 0, even_fade[h : h + 1], even_fade[half + h : half + h + 1])
        back[h] = jnp.broadcast_to(row, back.shape[1:])

    span = jnp.zeros(total_ref.shape, F32)
    prior_ref[pl.ds(keep, half)] = jnp.zeros((half,) + prior_ref.shape[1:], F32)
    for hop in range(1, groups):

        @pl.when(group >= hop)
        def _():
            pair_copy(hop).wait_recv()
            factor = jnp.exp2(span)
            for h in range(half):
                row = jnp.where(place == 0, factor[h : h + 1], factor[half + h : half + h + 1])
                prior_ref[keep + h] += row * pairs[hop - 1, h].astype(F32)

        source = lax.rem(group - hop + groups, groups) * 2
        span += total_of(source) + total_of(source + 1)

    for hop in range(1, groups):

        @pl.when(group + hop < groups)
        def _():
            pair_copy(hop).wait_send()

    for h in range(half):
        before = prior_ref[keep + h]
        later = back[h] * before + start[h]
        sent[h] = (odd * before + (1.0 - odd) * later).astype(BF16)
        prior_ref[keep + h] = odd * later + (1.0 - odd) * before
    answer = pltpu.make_async_remote_copy(
        src_ref=sent, dst_ref=landed, send_sem=back_sems.at[0], recv_sem=back_sems.at[1],
        device_id={"seq": partner}, device_id_type=MESH,
    )
    answer.start()
    answer.wait()
    prior_ref[pl.ds(give, half)] = landed[...].astype(F32)


def comm_params(number):
    return pltpu.CompilerParams(
        collective_id=number, has_side_effects=True, vmem_limit_bytes=VMEM_BYTES
    )


def carried_state(seq, end_state, totals, number):
    heads, size, width = end_state.shape
    half = heads // 2
    groups = seq // 2
    dma = pltpu.SemaphoreType.DMA
    whole = pl.BlockSpec(memory_space=pltpu.VMEM)
    return pl.pallas_call(
        functools.partial(prior_kernel, seq),
        out_shape=jax.ShapeDtypeStruct(end_state.shape, F32),
        in_specs=[whole, whole],
        out_specs=whole,
        scratch_shapes=[
            pltpu.VMEM((seq,) + totals.shape, F32),
            pltpu.VMEM((half, size, width), BF16),
            pltpu.VMEM((half, size, width), BF16),
            pltpu.VMEM((half, size, width), BF16),
            pltpu.VMEM((max(groups - 1, 1), half, size, width), BF16),
            pltpu.VMEM((half, size, width), F32),
            pltpu.VMEM((half, size, width), F32),
            pltpu.VMEM((half, size, width), BF16),
            dma((seq - 1,)),
            dma((seq - 1,)),
            dma((2,)),
            dma((max(groups - 1, 1),)),
            dma((max(groups - 1, 1),)),
            dma((2,)),
        ],
        compiler_params=comm_params(number),
        name=f"prior_{number}",
    )(end_state, totals)


def layer(seq, head, number, inputs, x_spec, gate, write_mat, read_mat, step_mat, decay_mat, skip):
    heads = step_mat.shape[0]
    size = write_mat.shape[0]
    blocks = step_mat.shape[1] // BLOCK
    features = gate.shape[-1]
    width = features // heads
    wide = pl.BlockSpec((size, BLOCK), lambda b: (0, b))
    thin = pl.BlockSpec((heads, BLOCK), lambda b: (0, b))
    rows = pl.BlockSpec((1, BLOCK, features), lambda b: (b, 0, 0))
    end_state, totals = pl.pallas_call(
        functools.partial(states_kernel, heads),
        grid=(blocks,),
        out_shape=(
            jax.ShapeDtypeStruct((heads, size, width), F32),
            jax.ShapeDtypeStruct((heads, LANES), F32),
        ),
        in_specs=[x_spec, wide, thin, thin],
        out_specs=(
            pl.BlockSpec((heads, size, width), lambda b: (0, 0, 0)),
            pl.BlockSpec((heads, LANES), lambda b: (0, 0)),
        ),
        name=f"states_{number}",
    )(inputs, write_mat, step_mat, decay_mat)
    prior = carried_state(seq, end_state, totals, number)
    gated, squares = pl.pallas_call(
        functools.partial(main_kernel, heads),
        grid=(blocks,),
        out_shape=(
            jax.ShapeDtypeStruct((blocks, BLOCK, features), BF16),
            jax.ShapeDtypeStruct((blocks, 8, BLOCK), F32),
        ),
        in_specs=[
            pl.BlockSpec(memory_space=pltpu.SMEM),
            x_spec,
            rows,
            wide,
            wide,
            thin,
            thin,
            pl.BlockSpec((heads, size, width), lambda b: (0, 0, 0)),
        ],
        out_specs=(rows, pl.BlockSpec((1, 8, BLOCK), lambda b: (b, 0, 0))),
        scratch_shapes=[pltpu.VMEM((heads, size, width), F32)],
        compiler_params=pltpu.CompilerParams(vmem_limit_bytes=VMEM_BYTES),
        name=f"main_{number}",
    )(skip, inputs, gate, write_mat, read_mat, step_mat, decay_mat, prior)
    whole = pl.BlockSpec(memory_space=pltpu.VMEM)
    squares = pl.pallas_call(
        functools.partial(sum_kernel, head),
        out_shape=jax.ShapeDtypeStruct(squares.shape, F32),
        in_specs=[whole],
        out_specs=whole,
        scratch_shapes=[
            pltpu.VMEM((head - 1,) + squares.shape, F32),
            pltpu.SemaphoreType.DMA((head - 1,)),
            pltpu.SemaphoreType.DMA((head - 1,)),
        ],
        compiler_params=comm_params(number + 2),
        name=f"squares_{number}",
    )(squares)
    return gated, squares


def normalise(head, gated, squares, gain, cols, out_shape, out_spec, number):
    features = gated.shape[-1]
    return pl.pallas_call(
        functools.partial(norm_kernel, features * head, cols),
        grid=(gated.shape[0],),
        out_shape=jax.ShapeDtypeStruct(out_shape, BF16),
        in_specs=[
            pl.BlockSpec((1, BLOCK, features), lambda b: (b, 0, 0)),
            pl.BlockSpec((1, 8, BLOCK), lambda b: (b, 0, 0)),
            pl.BlockSpec((1, features), lambda b: (0, 0)),
        ],
        out_specs=out_spec,
        compiler_params=pltpu.CompilerParams(vmem_limit_bytes=VMEM_BYTES),
        name=f"norm_{number}",
    )(gated, squares, gain.reshape(1, features))


def body(
    seq, head, tokens_in, gate_rows, gate_cols, write_rows, read_rows, step_rows, decay_rows,
    skip_rows, norm_rows, write_cols, read_cols, step_cols, decay_cols, skip_cols, norm_cols,
):
    grid_rows, grid_cols, features = tokens_in.shape
    blocks = grid_rows * grid_cols // BLOCK
    high = BLOCK // grid_cols
    local_cols = grid_cols // seq
    all_rows = grid_rows * seq
    per_col = all_rows // BLOCK
    slabs = BLOCK // grid_rows

    first = layer(
        seq, head, 0, tokens_in.reshape(blocks, BLOCK, features),
        pl.BlockSpec((1, BLOCK, features), lambda b: (b, 0, 0)),
        gate_rows.reshape(blocks, BLOCK, features),
        write_rows, read_rows, step_rows, decay_rows, skip_rows,
    )
    hidden = normalise(
        head, *first, norm_rows, grid_cols, (seq, local_cols, grid_rows, features),
        pl.BlockSpec((seq, local_cols, high, features), lambda b: (0, 0, b, 0)), 0,
    )
    anywhere = pl.BlockSpec(memory_space=pl.ANY)
    dma = pltpu.SemaphoreType.DMA
    hidden = pl.pallas_call(
        functools.partial(trade_kernel, seq),
        out_shape=jax.ShapeDtypeStruct(hidden.shape, BF16),
        in_specs=[anywhere],
        out_specs=anywhere,
        scratch_shapes=[dma((seq - 1,)), dma((seq - 1,)), dma(())],
        compiler_params=comm_params(4),
        name="trade",
    )(hidden)
    gate = jnp.transpose(gate_cols, (1, 0, 2)).reshape(local_cols * per_col, BLOCK, features)
    second = layer(
        seq, head, 1, hidden,
        pl.BlockSpec(
            (slabs, 1, grid_rows, features), lambda b: (b % per_col, b // per_col, 0, 0)
        ),
        gate, write_cols, read_cols, step_cols, decay_cols, skip_cols,
    )
    result = normalise(
        head, *second, norm_cols, 1, (local_cols * per_col, BLOCK, features),
        pl.BlockSpec((1, BLOCK, features), lambda b: (b, 0, 0)), 1,
    )
    return jnp.transpose(result.reshape(local_cols, all_rows, features), (1, 0, 2))


def solution(mesh):
    placed = (
        P("seq", None, "head"),
        P("seq", None, "head"),
        P(None, "seq", "head"),
        P(None, "seq"),
        P(None, "seq"),
        P("head", "seq"),
        P("head", "seq"),
        P("head"),
        P("head"),
        P(None, "seq"),
        P(None, "seq"),
        P("head", "seq"),
        P("head", "seq"),
        P("head"),
        P("head"),
    )
    return jax.shard_map(
        functools.partial(body, mesh.shape["seq"], mesh.shape["head"]),
        mesh=mesh, in_specs=placed, out_specs=P(None, "seq", "head"), check_vma=False,
    )
```

```python
import functools
import jax
import jax.numpy as jnp
from jax import lax
from jax.experimental import pallas as pl
from jax.experimental.pallas import tpu as pltpu
from jax.sharding import PartitionSpec as P

BLOCK = 256
LANES = 128
EPSILON = 1e-05
LOG2E = 1.4426950408889634
HIGHEST = lax.Precision.HIGHEST
MESH = pl.DeviceIdType.MESH
F32 = jnp.float32
BF16 = jnp.bfloat16
VMEM_BYTES = 60 * 1024 * 1024


def contract(a, b, dims, precision=None):
    return lax.dot_general(
        a, b, (dims, ((), ())), precision=precision, preferred_element_type=F32
    )


def iota(shape, axis):
    return lax.broadcasted_iota(jnp.int32, shape, axis)


def block_sums(decay):
    upper = (iota((BLOCK, BLOCK), 0) <= iota((BLOCK, BLOCK), 1)).astype(F32)
    cumulative = contract(decay, upper, ((1,), (0,)), HIGHEST)
    total = contract(decay, jnp.ones((BLOCK, LANES), F32), ((1,), (0,)), HIGHEST)
    return cumulative, total


def head_state(write32, weight_row, tokens):
    loaded = (write32 * weight_row).astype(BF16)
    return contract(loaded, tokens, ((1,), (0,)))


def column_scale(local_cols, per_col, grid_rows, grid_cols, place_ref, scales):
    high = BLOCK // grid_cols
    column = place_ref[0] * local_cols + pl.program_id(0) // per_col
    shape = (BLOCK, scales.shape[0])
    row = iota(shape, 0)
    depth = scales.shape[0] * grid_rows // BLOCK
    source = (row // grid_rows) * depth + (row % grid_rows) // high
    picked = contract((iota(shape, 1) == source).astype(F32), scales, ((1,), (0,)), HIGHEST)
    lane = (iota((BLOCK, BLOCK), 0) % high) * grid_cols + column
    return jnp.sum(jnp.where(iota((BLOCK, BLOCK), 1) == lane, picked, 0.0), axis=1, keepdims=True)


def states_kernel(heads, scale_of, *refs):
    if scale_of is None:
        x_ref, write_ref, step_ref, decay_ref, end_ref, total_ref = refs
    else:
        (place_ref, scales_ref, gain_ref, x_ref, write_ref, step_ref, decay_ref, end_ref,
         total_ref, hidden_ref) = refs
    step_at = pl.program_id(0)

    @pl.when(step_at == 0)
    def _():
        end_ref[...] = jnp.zeros_like(end_ref)
        total_ref[...] = jnp.zeros_like(total_ref)

    cumulative, total = block_sums(decay_ref[...] * LOG2E)
    tokens = x_ref[...].reshape(BLOCK, x_ref.shape[-1])
    if scale_of is not None:
        scale = scale_of(place_ref, scales_ref[...])
    write32 = write_ref[...].astype(F32)
    final = total[:, :1]
    weights = jnp.exp2(final - cumulative) * step_ref[...]
    fade = jnp.exp2(total)
    for h in range(heads):
        lanes = slice(h * LANES, (h + 1) * LANES)
        own = tokens[:, lanes]
        if scale_of is not None:
            own = (own.astype(F32) * scale * gain_ref[:, lanes]).astype(BF16)
            hidden_ref[0, :, lanes] = own
        gained = head_state(write32, weights[h : h + 1], own)
        end_ref[h] = fade[h : h + 1] * end_ref[h] + gained
    total_ref[...] += total


def main_kernel(
    heads, cols, skip_ref, x_ref, gate_ref, write_ref, read_ref, step_ref, decay_ref, prior_ref,
    gated_ref, squares_ref, state,
):
    @pl.when(pl.program_id(0) == 0)
    def _():
        state[...] = prior_ref[...]
        squares_ref[...] = jnp.zeros_like(squares_ref)

    decay = decay_ref[...] * LOG2E
    step = step_ref[...]
    cumulative, total = block_sums(decay)
    lower = (iota((BLOCK, BLOCK), 0) >= iota((BLOCK, BLOCK), 1)).astype(F32)
    across = contract(lower, decay, ((1,), (1,)), HIGHEST)
    lifting = jnp.exp2(across)
    tokens = x_ref[...].reshape(BLOCK, x_ref.shape[-1])
    write = write_ref[...]
    read = read_ref[...]
    write32 = write.astype(F32)
    scores = contract(read, write, ((0,), (0,))) * lower
    weights = jnp.exp2(total[:, :1] - cumulative) * step
    fade = jnp.exp2(total)
    squares = jnp.zeros((BLOCK, LANES), F32)
    read_twice = jnp.concatenate([read, read], axis=0)
    high = BLOCK // cols
    to = iota((BLOCK, BLOCK), 0)
    chosen = ((to % high) * cols + to // high == iota((BLOCK, BLOCK), 1)).astype(BF16)
    for h in range(heads):
        lanes = slice(h * LANES, (h + 1) * LANES)
        own = tokens[:, lanes]
        spread = jnp.minimum(across[:, h : h + 1] - cumulative[h : h + 1], 0.0)
        mixing = (jnp.exp2(spread) * scores * step[h : h + 1]).astype(BF16)
        held = state[h]
        out = contract(mixing, own, ((1,), (0,)))
        coarse = held.astype(BF16)
        fine = (held - coarse.astype(F32)).astype(BF16)
        parts = jnp.concatenate([coarse, fine], axis=0)
        out += lifting[:, h : h + 1] * contract(read_twice, parts, ((0,), (0,)))
        out += skip_ref[h] * own.astype(F32)
        gate = gate_ref[0, :, lanes].astype(F32)
        gated = out * (gate / (1.0 + jnp.exp2(gate * -LOG2E)))
        squares += gated * gated
        if cols > 1:
            moved = contract(chosen, gated.astype(BF16), ((1,), (0,)))
            gated_ref[:, :, :, lanes] = moved.reshape(gated_ref.shape[:3] + (LANES,)).astype(BF16)
        else:
            gated_ref[0, :, lanes] = gated
        state[h] = fade[h : h + 1] * held + head_state(write32, weights[h : h + 1], own)
    row = contract(jnp.ones((8, LANES), F32), squares, ((1,), (1,)), HIGHEST)
    squares_ref[pl.ds(pl.program_id(0), 1), :] = row[:1]


def norm_kernel(inner, per_col, gated_ref, squares_ref, gain_ref, out_ref):
    cols, rows, features = gated_ref.shape
    square = (BLOCK, BLOCK)
    start = pl.program_id(0) * rows
    lane = start % BLOCK + iota(square, 0) % rows
    sums = contract((lane == iota(square, 1)).astype(F32), squares_ref[...], ((1,), (1,)), HIGHEST)
    block = (iota(sums.shape, 0) // rows) * per_col + start // BLOCK
    sums = jnp.sum(jnp.where(iota(sums.shape, 1) == block, sums, 0.0), axis=1, keepdims=True)
    scaled = lax.rsqrt(sums / inner + EPSILON)
    chosen = ((iota(square, 0) % cols) * rows + iota(square, 0) // cols == iota(square, 1)).astype(BF16)
    for at in range(0, features, LANES):
        lanes = slice(at, at + LANES)
        result = gated_ref[:, :, lanes].reshape(BLOCK, LANES) * scaled * gain_ref[:, lanes]
        result = result.astype(BF16)
        if cols > 1:
            moved = contract(chosen, result, ((1,), (0,)))
            out_ref[:, :, lanes] = moved.reshape(rows, cols, LANES).astype(BF16)
        else:
            out_ref[:, lanes] = result


def greet(axes):
    barrier = pltpu.get_barrier_semaphore()
    for axis, count in axes:
        me = lax.axis_index(axis)
        for hop in range(1, count):
            pl.semaphore_signal(
                barrier, inc=1, device_id={axis: lax.rem(me + hop, count)}, device_id_type=MESH
            )
    pl.semaphore_wait(barrier, sum(count - 1 for _, count in axes))


def head_sum(count, own_ref, held, send_sems, recv_sems):
    me = lax.axis_index("head")
    copies = []
    for hop in range(1, count):
        copy = pltpu.make_async_remote_copy(
            src_ref=own_ref,
            dst_ref=held.at[hop - 1],
            send_sem=send_sems.at[hop - 1],
            recv_sem=recv_sems.at[hop - 1],
            device_id={"head": lax.rem(me + hop, count)},
            device_id_type=MESH,
        )
        copy.start()
        copies.append(copy)
    for copy in copies:
        copy.wait()
    total = own_ref[...]
    for hop in range(1, count):
        total += held[hop - 1]
    return total


def sum_kernel(count, own_ref, out_ref, held, send_sems, recv_sems):
    greet((("head", count),))
    out_ref[...] = head_sum(count, own_ref, held, send_sems, recv_sems)


def trade_kernel(
    count, heads, inner, own_ref, squares_ref, out_ref, scales_ref, held, scale, sum_send,
    sum_recv, scale_send, scale_recv, send_sems, recv_sems, local_sem,
):
    greet((("seq", count), ("head", heads)))
    me = lax.axis_index("seq")
    copies = []
    for hop in range(count // 2, count // 2 + count - 1):
        ahead = 1 + (hop - 1) % (count - 1)
        to = lax.rem(me + ahead, count)
        copy = pltpu.make_async_remote_copy(
            src_ref=own_ref.at[to],
            dst_ref=out_ref.at[me],
            send_sem=send_sems.at[ahead - 1],
            recv_sem=recv_sems.at[ahead - 1],
            device_id={"seq": to},
            device_id_type=MESH,
        )
        copy.start()
        copies.append(copy)
    local = pltpu.make_async_copy(own_ref.at[me], out_ref.at[me], local_sem)
    local.start()
    total = head_sum(heads, squares_ref, held, sum_send, sum_recv)
    scale[...] = lax.rsqrt(total / inner + EPSILON)
    depth = scale.shape[0]
    mine = pl.ds(pl.multiple_of(me * depth, depth), depth)
    for hop in range(1, count):
        copy = pltpu.make_async_remote_copy(
            src_ref=scale,
            dst_ref=scales_ref.at[mine],
            send_sem=scale_send.at[hop - 1],
            recv_sem=scale_recv.at[hop - 1],
            device_id={"seq": lax.rem(me + hop, count)},
            device_id_type=MESH,
        )
        copy.start()
        copies.append(copy)
    scales_ref[mine, :] = scale[...]
    local.wait()
    for copy in copies:
        copy.wait()


def prior_kernel(
    count, end_ref, total_ref, prior_ref, totals, sent, swapped, pair, pairs, back, start, landed, near,
    near_sems, total_send, total_recv, swap_sems, pair_send, pair_recv, back_sems,
):
    heads = end_ref.shape[0]
    half = heads // 2
    greet((("seq", count),))
    me = lax.axis_index("seq")
    place = lax.rem(me, 2)
    partner = me + 1 - 2 * place
    group = me // 2
    groups = count // 2
    keep = place * half
    give = half - keep

    sent[...] = end_ref[pl.ds(give, half)].astype(BF16)
    swap = pltpu.make_async_remote_copy(
        src_ref=sent, dst_ref=swapped, send_sem=swap_sems.at[0], recv_sem=swap_sems.at[1],
        device_id={"seq": partner}, device_id_type=MESH,
    )
    swap.start()
    near_copy = pltpu.make_async_remote_copy(
        src_ref=total_ref, dst_ref=near, send_sem=near_sems.at[0], recv_sem=near_sems.at[1],
        device_id={"seq": partner}, device_id_type=MESH,
    )
    near_copy.start()
    total_copies = []
    for hop in range(1, count):
        copy = pltpu.make_async_remote_copy(
            src_ref=total_ref, dst_ref=totals.at[hop], send_sem=total_send.at[hop - 1],
            recv_sem=total_recv.at[hop - 1],
            device_id={"seq": lax.rem(me + hop, count)}, device_id_type=MESH,
        )
        copy.start()
        total_copies.append(copy)
    totals[0] = total_ref[...]
    near_copy.wait()
    swap.wait()

    def total_of(device):
        return totals[lax.rem(me - device + count, count)]

    odd = place.astype(F32)
    odd_fade = jnp.exp2(jnp.where(place == 0, near[...], total_ref[...]))
    even_fade = jnp.exp2(jnp.where(place == 0, total_ref[...], near[...]))
    for h in range(half):
        mine = end_ref[keep + h]
        other = swapped[h].astype(F32)
        first = odd * other + (1.0 - odd) * mine
        last = odd * mine + (1.0 - odd) * other
        row = jnp.where(place == 0, odd_fade[h : h + 1], odd_fade[half + h : half + h + 1])
        pair[h] = (row * first + last).astype(BF16)
        start[h] = first

    def pair_copy(hop):
        return pltpu.make_async_remote_copy(
            src_ref=pair, dst_ref=pairs.at[hop - 1], send_sem=pair_send.at[hop - 1],
            recv_sem=pair_recv.at[hop - 1],
            device_id={"seq": lax.rem(me + 2 * hop, count)}, device_id_type=MESH,
        )

    for hop in range(1, groups):

        @pl.when(group + hop < groups)
        def _():
            pair_copy(hop).start()

    for h in range(half):
        row = jnp.where(place == 0, even_fade[h : h + 1], even_fade[half + h : half + h + 1])
        back[h] = jnp.broadcast_to(row, back.shape[1:])

    for copy in total_copies:
        copy.wait()
    span = jnp.zeros(total_ref.shape, F32)
    prior_ref[pl.ds(keep, half)] = jnp.zeros((half,) + prior_ref.shape[1:], F32)
    for hop in range(1, groups):

        @pl.when(group >= hop)
        def _():
            pair_copy(hop).wait_recv()
            factor = jnp.exp2(span)
            for h in range(half):
                row = jnp.where(place == 0, factor[h : h + 1], factor[half + h : half + h + 1])
                prior_ref[keep + h] += row * pairs[hop - 1, h].astype(F32)

        source = lax.rem(group - hop + groups, groups) * 2
        span += total_of(source) + total_of(source + 1)

    for hop in range(1, groups):

        @pl.when(group + hop < groups)
        def _():
            pair_copy(hop).wait_send()

    for h in range(half):
        before = prior_ref[keep + h]
        later = back[h] * before + start[h]
        sent[h] = (odd * before + (1.0 - odd) * later).astype(BF16)
        prior_ref[keep + h] = odd * later + (1.0 - odd) * before
    answer = pltpu.make_async_remote_copy(
        src_ref=sent, dst_ref=landed, send_sem=back_sems.at[0], recv_sem=back_sems.at[1],
        device_id={"seq": partner}, device_id_type=MESH,
    )
    answer.start()
    answer.wait()
    prior_ref[pl.ds(give, half)] = landed[...].astype(F32)


def comm_params(number):
    return pltpu.CompilerParams(
        collective_id=number, has_side_effects=True, vmem_limit_bytes=VMEM_BYTES
    )


def carried_state(seq, end_state, totals, number):
    heads, size, width = end_state.shape
    half = heads // 2
    groups = seq // 2
    dma = pltpu.SemaphoreType.DMA
    whole = pl.BlockSpec(memory_space=pltpu.VMEM)
    return pl.pallas_call(
        functools.partial(prior_kernel, seq),
        out_shape=jax.ShapeDtypeStruct(end_state.shape, F32),
        in_specs=[whole, whole],
        out_specs=whole,
        scratch_shapes=[
            pltpu.VMEM((seq,) + totals.shape, F32),
            pltpu.VMEM((half, size, width), BF16),
            pltpu.VMEM((half, size, width), BF16),
            pltpu.VMEM((half, size, width), BF16),
            pltpu.VMEM((max(groups - 1, 1), half, size, width), BF16),
            pltpu.VMEM((half, size, width), F32),
            pltpu.VMEM((half, size, width), F32),
            pltpu.VMEM((half, size, width), BF16),
            pltpu.VMEM(totals.shape, F32),
            dma((2,)),
            dma((seq - 1,)),
            dma((seq - 1,)),
            dma((2,)),
            dma((max(groups - 1, 1),)),
            dma((max(groups - 1, 1),)),
            dma((2,)),
        ],
        compiler_params=comm_params(number),
        name=f"prior_{number}",
    )(end_state, totals)


def layer(
    seq, number, inputs, x_spec, gate, write_mat, read_mat, step_mat, decay_mat, skip, cols,
    out, out_spec, norm_of=None,
):
    heads = step_mat.shape[0]
    size = write_mat.shape[0]
    blocks = step_mat.shape[1] // BLOCK
    features = gate.shape[-1]
    width = features // heads
    wide = pl.BlockSpec((size, BLOCK), lambda b: (0, b))
    thin = pl.BlockSpec((heads, BLOCK), lambda b: (0, b))
    rows = pl.BlockSpec((1, BLOCK, features), lambda b: (b, 0, 0))
    params = pltpu.CompilerParams(vmem_limit_bytes=VMEM_BYTES)
    scale_of, extra, extra_specs = None, (), []
    shapes = [
        jax.ShapeDtypeStruct((heads, size, width), F32),
        jax.ShapeDtypeStruct((heads, LANES), F32),
    ]
    specs = [
        pl.BlockSpec((heads, size, width), lambda b: (0, 0, 0)),
        pl.BlockSpec((heads, LANES), lambda b: (0, 0)),
    ]
    if norm_of is not None:
        scale_of, extra, extra_specs = norm_of
        shapes.append(jax.ShapeDtypeStruct((blocks, BLOCK, features), BF16))
        specs.append(rows)
    made = pl.pallas_call(
        functools.partial(states_kernel, heads, scale_of),
        grid=(blocks,),
        out_shape=shapes,
        in_specs=[*extra_specs, x_spec, wide, thin, thin],
        out_specs=specs,
        compiler_params=params,
        name=f"states_{number}",
    )(*extra, inputs, write_mat, step_mat, decay_mat)
    prior = carried_state(seq, made[0], made[1], number)
    if norm_of is not None:
        inputs, x_spec = made[2], rows
    depth = -(-blocks // 8) * 8
    return pl.pallas_call(
        functools.partial(main_kernel, heads, cols),
        grid=(blocks,),
        out_shape=(out, jax.ShapeDtypeStruct((depth, BLOCK), F32)),
        in_specs=[
            pl.BlockSpec(memory_space=pltpu.SMEM),
            x_spec,
            rows,
            wide,
            wide,
            thin,
            thin,
            pl.BlockSpec((heads, size, width), lambda b: (0, 0, 0)),
        ],
        out_specs=(out_spec, pl.BlockSpec((depth, BLOCK), lambda b: (0, 0))),
        scratch_shapes=[pltpu.VMEM((heads, size, width), F32)],
        compiler_params=params,
        name=f"main_{number}",
    )(skip, inputs, gate, write_mat, read_mat, step_mat, decay_mat, prior)


def body(
    seq, head, tokens_in, gate_rows, gate_cols, write_rows, read_rows, step_rows, decay_rows,
    skip_rows, norm_rows, write_cols, read_cols, step_cols, decay_cols, skip_cols, norm_cols,
):
    grid_rows, grid_cols, features = tokens_in.shape
    blocks = grid_rows * grid_cols // BLOCK
    high = BLOCK // grid_cols
    local_cols = grid_cols // seq
    all_rows = grid_rows * seq
    per_col = all_rows // BLOCK
    slabs = BLOCK // grid_rows
    inner = features * head
    dma = pltpu.SemaphoreType.DMA
    anywhere = pl.BlockSpec(memory_space=pl.ANY)
    whole = pl.BlockSpec(memory_space=pltpu.VMEM)
    rows = pl.BlockSpec((1, BLOCK, features), lambda b: (b, 0, 0))

    gated, squares = layer(
        seq, 0, tokens_in.reshape(blocks, BLOCK, features), rows,
        gate_rows.reshape(blocks, BLOCK, features),
        write_rows, read_rows, step_rows, decay_rows, skip_rows, grid_cols,
        jax.ShapeDtypeStruct((seq, local_cols, grid_rows, features), BF16),
        pl.BlockSpec((seq, local_cols, high, features), lambda b: (0, 0, b, 0)),
    )
    depth = squares.shape[0]
    hidden, scales = pl.pallas_call(
        functools.partial(trade_kernel, seq, head, inner),
        out_shape=(
            jax.ShapeDtypeStruct(gated.shape, BF16),
            jax.ShapeDtypeStruct((seq * depth, BLOCK), F32),
        ),
        in_specs=[anywhere, whole],
        out_specs=(anywhere, whole),
        scratch_shapes=[
            pltpu.VMEM((head - 1,) + squares.shape, F32),
            pltpu.VMEM(squares.shape, F32),
            dma((head - 1,)), dma((head - 1,)),
            dma((seq - 1,)), dma((seq - 1,)),
            dma((seq - 1,)), dma((seq - 1,)), dma(()),
        ],
        compiler_params=comm_params(2),
        name="trade",
    )(gated, squares)
    gate = jnp.transpose(gate_cols, (1, 0, 2)).reshape(local_cols * per_col, BLOCK, features)
    gated, squares = layer(
        seq, 1, hidden,
        pl.BlockSpec(
            (slabs, 1, grid_rows, features), lambda b: (b % per_col, b // per_col, 0, 0)
        ),
        gate, write_cols, read_cols, step_cols, decay_cols, skip_cols, 1,
        jax.ShapeDtypeStruct((local_cols * per_col, BLOCK, features), F32), rows,
        (
            functools.partial(column_scale, local_cols, per_col, grid_rows, grid_cols),
            (lax.axis_index("seq").reshape(1), scales, norm_rows.reshape(1, features)),
            [
                pl.BlockSpec(memory_space=pltpu.SMEM),
                pl.BlockSpec((slabs * depth, BLOCK), lambda b: (b % per_col, 0)),
                pl.BlockSpec((1, features), lambda b: (0, 0)),
            ],
        ),
    )
    squares = pl.pallas_call(
        functools.partial(sum_kernel, head),
        out_shape=jax.ShapeDtypeStruct(squares.shape, F32),
        in_specs=[whole],
        out_specs=whole,
        scratch_shapes=[
            pltpu.VMEM((head - 1,) + squares.shape, F32), dma((head - 1,)), dma((head - 1,)),
        ],
        compiler_params=comm_params(3),
        name="squares",
    )(squares)
    part = BLOCK // local_cols
    out_shape, out_spec = (all_rows, local_cols, features), (part, local_cols, features)
    if local_cols == 1:
        out_shape, out_spec = (all_rows, features), (part, features)
    result = pl.pallas_call(
        functools.partial(norm_kernel, inner, per_col),
        grid=(all_rows // part,),
        out_shape=jax.ShapeDtypeStruct(out_shape, BF16),
        in_specs=[
            pl.BlockSpec((local_cols, part, features), lambda q: (0, q, 0)),
            pl.BlockSpec(squares.shape, lambda q: (0, 0)),
            pl.BlockSpec((1, features), lambda q: (0, 0)),
        ],
        out_specs=pl.BlockSpec(out_spec, lambda q: (q,) + (0,) * (len(out_spec) - 1)),
        compiler_params=pltpu.CompilerParams(vmem_limit_bytes=VMEM_BYTES),
        name="norm",
    )(gated.reshape(local_cols, all_rows, features), squares, norm_cols.reshape(1, features))
    return result.reshape(all_rows, local_cols, features)


def solution(mesh):
    placed = (
        P("seq", None, "head"),
        P("seq", None, "head"),
        P(None, "seq", "head"),
        P(None, "seq"),
        P(None, "seq"),
        P("head", "seq"),
        P("head", "seq"),
        P("head"),
        P("head"),
        P(None, "seq"),
        P(None, "seq"),
        P("head", "seq"),
        P("head", "seq"),
        P("head"),
        P("head"),
    )
    return jax.shard_map(
        functools.partial(body, mesh.shape["seq"], mesh.shape["head"]),
        mesh=mesh, in_specs=placed, out_specs=P(None, "seq", "head"), check_vma=False,
    )
```

```python
import functools
import jax
import jax.numpy as jnp
from jax import lax
from jax.experimental import pallas as pl
from jax.experimental.pallas import tpu as pltpu
from jax.sharding import PartitionSpec as P

BLOCK = 256
LANES = 128
EPSILON = 1e-05
LOG2E = 1.4426950408889634
HIGHEST = lax.Precision.HIGHEST
MESH = pl.DeviceIdType.MESH
F32 = jnp.float32
BF16 = jnp.bfloat16
VMEM_BYTES = 60 * 1024 * 1024


def contract(a, b, dims, precision=None):
    return lax.dot_general(
        a, b, (dims, ((), ())), precision=precision, preferred_element_type=F32
    )


def iota(shape, axis):
    return lax.broadcasted_iota(jnp.int32, shape, axis)


def block_sums(decay):
    upper = (iota((BLOCK, BLOCK), 0) <= iota((BLOCK, BLOCK), 1)).astype(F32)
    cumulative = contract(decay, upper, ((1,), (0,)), HIGHEST)
    total = contract(decay, jnp.ones((BLOCK, LANES), F32), ((1,), (0,)), HIGHEST)
    return cumulative, total


def head_state(write32, weight_row, tokens):
    loaded = (write32 * weight_row).astype(BF16)
    return contract(loaded, tokens, ((1,), (0,)))


def column_scale(local_cols, per_col, grid_rows, grid_cols, place_ref, scales):
    high = BLOCK // grid_cols
    column = place_ref[0] * local_cols + pl.program_id(0) // per_col
    shape = (BLOCK, scales.shape[0])
    row = iota(shape, 0)
    depth = scales.shape[0] * grid_rows // BLOCK
    source = (row // grid_rows) * depth + (row % grid_rows) // high
    picked = contract((iota(shape, 1) == source).astype(F32), scales, ((1,), (0,)), HIGHEST)
    lane = (iota((BLOCK, BLOCK), 0) % high) * grid_cols + column
    return jnp.sum(jnp.where(iota((BLOCK, BLOCK), 1) == lane, picked, 0.0), axis=1, keepdims=True)


def states_kernel(heads, scale_of, *refs):
    if scale_of is None:
        x_ref, write_ref, step_ref, decay_ref, end_ref, total_ref = refs
    else:
        (place_ref, scales_ref, gain_ref, x_ref, write_ref, step_ref, decay_ref, end_ref,
         total_ref, hidden_ref) = refs
    step_at = pl.program_id(0)

    @pl.when(step_at == 0)
    def _():
        end_ref[...] = jnp.zeros_like(end_ref)
        total_ref[...] = jnp.zeros_like(total_ref)

    cumulative, total = block_sums(decay_ref[...] * LOG2E)
    tokens = x_ref[...].reshape(BLOCK, x_ref.shape[-1])
    if scale_of is not None:
        scale = scale_of(place_ref, scales_ref[...])
    write32 = write_ref[...].astype(F32)
    final = total[:, :1]
    weights = jnp.exp2(final - cumulative) * step_ref[...]
    fade = jnp.exp2(total)
    for h in range(heads):
        lanes = slice(h * LANES, (h + 1) * LANES)
        own = tokens[:, lanes]
        if scale_of is not None:
            own = (own.astype(F32) * scale * gain_ref[:, lanes]).astype(BF16)
            hidden_ref[0, :, lanes] = own
        gained = head_state(write32, weights[h : h + 1], own)
        end_ref[h] = fade[h : h + 1] * end_ref[h] + gained
    total_ref[...] += total


def main_kernel(
    heads, cols, skip_ref, x_ref, gate_ref, write_ref, read_ref, step_ref, decay_ref, prior_ref,
    gated_ref, squares_ref, state, turned,
):
    @pl.when(pl.program_id(0) == 0)
    def _():
        state[...] = prior_ref[...]
        squares_ref[...] = jnp.zeros_like(squares_ref)

    decay = decay_ref[...] * LOG2E
    step = step_ref[...]
    cumulative, total = block_sums(decay)
    lower = (iota((BLOCK, BLOCK), 0) >= iota((BLOCK, BLOCK), 1)).astype(F32)
    across = contract(lower, decay, ((1,), (1,)), HIGHEST)
    lifting = jnp.exp2(across)
    tokens = x_ref[...].reshape(BLOCK, x_ref.shape[-1])
    write = write_ref[...]
    read = read_ref[...]
    write32 = write.astype(F32)
    scores = contract(read, write, ((0,), (0,))) * lower
    weights = jnp.exp2(total[:, :1] - cumulative) * step
    fade = jnp.exp2(total)
    squares = jnp.zeros((BLOCK, LANES), F32)
    read_twice = jnp.concatenate([read, read], axis=0)
    high = BLOCK // cols
    for h in range(heads):
        lanes = slice(h * LANES, (h + 1) * LANES)
        own = tokens[:, lanes]
        spread = jnp.minimum(across[:, h : h + 1] - cumulative[h : h + 1], 0.0)
        mixing = (jnp.exp2(spread) * scores * step[h : h + 1]).astype(BF16)
        held = state[h]
        loaded = (write32 * weights[h : h + 1]).astype(BF16)
        both = contract(jnp.concatenate([mixing, loaded], axis=0), own, ((1,), (0,)))
        out = both[:BLOCK]
        if h % 2 == 0:
            pair = jnp.concatenate([held] + ([state[h + 1]] if h + 1 < heads else []), axis=1)
            coarse = pair.astype(BF16)
            fine = (pair - coarse.astype(F32)).astype(BF16)
            parts = jnp.concatenate([coarse, fine], axis=0)
            from_state = contract(read_twice, parts, ((0,), (0,)))
        side = (h % 2) * LANES
        out += lifting[:, h : h + 1] * from_state[:, side : side + LANES]
        out += skip_ref[h] * own.astype(F32)
        gate = gate_ref[0, :, lanes].astype(F32)
        gated = out * (gate / (1.0 + jnp.exp2(gate * -LOG2E)))
        squares += gated * gated
        if cols > 1:
            near = gated_ref.shape[1]
            slot = turned.at[h % 2]
            slot[...] = gated
            for c in range(cols):
                gated_ref[c // near, c % near, :, lanes] = slot[
                    pl.ds(c, high, stride=cols), :
                ].astype(BF16)
        else:
            gated_ref[0, :, lanes] = gated
        state[h] = fade[h : h + 1] * held + both[BLOCK:]
    row = contract(jnp.ones((8, LANES), F32), squares, ((1,), (1,)), HIGHEST)
    squares_ref[pl.ds(pl.program_id(0), 1), :] = row[:1]


def norm_kernel(inner, per_col, gated_ref, squares_ref, gain_ref, out_ref, turned):
    cols, rows, features = gated_ref.shape
    square = (BLOCK, BLOCK)
    start = pl.program_id(0) * rows
    lane = start % BLOCK + iota(square, 0) % rows
    sums = contract((lane == iota(square, 1)).astype(F32), squares_ref[...], ((1,), (1,)), HIGHEST)
    block = (iota(sums.shape, 0) // rows) * per_col + start // BLOCK
    sums = jnp.sum(jnp.where(iota(sums.shape, 1) == block, sums, 0.0), axis=1, keepdims=True)
    scaled = lax.rsqrt(sums / inner + EPSILON)
    for at in range(0, features, LANES):
        lanes = slice(at, at + LANES)
        result = gated_ref[:, :, lanes].reshape(BLOCK, LANES) * scaled * gain_ref[:, lanes]
        if cols > 1:
            slot = turned.at[at // LANES % 2]
            for c in range(cols):
                slot[pl.ds(c, rows, stride=cols), :] = result[c * rows : (c + 1) * rows]
            out_ref[:, :, lanes] = slot[...].reshape(rows, cols, LANES).astype(BF16)
        else:
            out_ref[:, lanes] = result.astype(BF16)


def greet(axes):
    barrier = pltpu.get_barrier_semaphore()
    for axis, count in axes:
        me = lax.axis_index(axis)
        for hop in range(1, count):
            pl.semaphore_signal(
                barrier, inc=1, device_id={axis: lax.rem(me + hop, count)}, device_id_type=MESH
            )
    pl.semaphore_wait(barrier, sum(count - 1 for _, count in axes))


def head_sum(count, own_ref, held, send_sems, recv_sems):
    me = lax.axis_index("head")
    copies = []
    for hop in range(1, count):
        copy = pltpu.make_async_remote_copy(
            src_ref=own_ref,
            dst_ref=held.at[hop - 1],
            send_sem=send_sems.at[hop - 1],
            recv_sem=recv_sems.at[hop - 1],
            device_id={"head": lax.rem(me + hop, count)},
            device_id_type=MESH,
        )
        copy.start()
        copies.append(copy)
    for copy in copies:
        copy.wait()
    total = own_ref[...]
    for hop in range(1, count):
        total += held[hop - 1]
    return total


def sum_kernel(count, own_ref, out_ref, held, send_sems, recv_sems):
    greet((("head", count),))
    out_ref[...] = head_sum(count, own_ref, held, send_sems, recv_sems)


def trade_kernel(
    count, heads, inner, own_ref, squares_ref, out_ref, scales_ref, held, scale, sum_send,
    sum_recv, scale_send, scale_recv, send_sems, recv_sems, local_sem,
):
    greet((("seq", count), ("head", heads)))
    me = lax.axis_index("seq")
    copies = []
    for hop in range(count // 2, count // 2 + count - 1):
        ahead = 1 + (hop - 1) % (count - 1)
        to = lax.rem(me + ahead, count)
        copy = pltpu.make_async_remote_copy(
            src_ref=own_ref.at[to],
            dst_ref=out_ref.at[me],
            send_sem=send_sems.at[ahead - 1],
            recv_sem=recv_sems.at[ahead - 1],
            device_id={"seq": to},
            device_id_type=MESH,
        )
        copy.start()
        copies.append(copy)
    local = pltpu.make_async_copy(own_ref.at[me], out_ref.at[me], local_sem)
    local.start()
    total = head_sum(heads, squares_ref, held, sum_send, sum_recv)
    scale[...] = lax.rsqrt(total / inner + EPSILON)
    depth = scale.shape[0]
    mine = pl.ds(pl.multiple_of(me * depth, depth), depth)
    for hop in range(1, count):
        copy = pltpu.make_async_remote_copy(
            src_ref=scale,
            dst_ref=scales_ref.at[mine],
            send_sem=scale_send.at[hop - 1],
            recv_sem=scale_recv.at[hop - 1],
            device_id={"seq": lax.rem(me + hop, count)},
            device_id_type=MESH,
        )
        copy.start()
        copies.append(copy)
    scales_ref[mine, :] = scale[...]
    local.wait()
    for copy in copies:
        copy.wait()


def prior_kernel(
    count, end_ref, total_ref, prior_ref, totals, sent, swapped, pair, pairs, back, start, landed, near,
    near_sems, total_send, total_recv, swap_sems, pair_send, pair_recv, back_sems,
):
    heads = end_ref.shape[0]
    half = heads // 2
    greet((("seq", count),))
    me = lax.axis_index("seq")
    place = lax.rem(me, 2)
    partner = me + 1 - 2 * place
    group = me // 2
    groups = count // 2
    keep = place * half
    give = half - keep

    sent[...] = end_ref[pl.ds(give, half)].astype(BF16)
    swap = pltpu.make_async_remote_copy(
        src_ref=sent, dst_ref=swapped, send_sem=swap_sems.at[0], recv_sem=swap_sems.at[1],
        device_id={"seq": partner}, device_id_type=MESH,
    )
    swap.start()
    near_copy = pltpu.make_async_remote_copy(
        src_ref=total_ref, dst_ref=near, send_sem=near_sems.at[0], recv_sem=near_sems.at[1],
        device_id={"seq": partner}, device_id_type=MESH,
    )
    near_copy.start()
    total_copies = []
    for hop in range(1, count):
        copy = pltpu.make_async_remote_copy(
            src_ref=total_ref, dst_ref=totals.at[hop], send_sem=total_send.at[hop - 1],
            recv_sem=total_recv.at[hop - 1],
            device_id={"seq": lax.rem(me + hop, count)}, device_id_type=MESH,
        )
        copy.start()
        total_copies.append(copy)
    totals[0] = total_ref[...]
    near_copy.wait()
    swap.wait()

    def total_of(device):
        return totals[lax.rem(me - device + count, count)]

    odd = place.astype(F32)
    odd_fade = jnp.exp2(jnp.where(place == 0, near[...], total_ref[...]))
    even_fade = jnp.exp2(jnp.where(place == 0, total_ref[...], near[...]))
    for h in range(half):
        mine = end_ref[keep + h]
        other = swapped[h].astype(F32)
        first = odd * other + (1.0 - odd) * mine
        last = odd * mine + (1.0 - odd) * other
        row = jnp.where(place == 0, odd_fade[h : h + 1], odd_fade[half + h : half + h + 1])
        pair[h] = (row * first + last).astype(BF16)
        start[h] = first

    def pair_copy(hop):
        return pltpu.make_async_remote_copy(
            src_ref=pair, dst_ref=pairs.at[hop - 1], send_sem=pair_send.at[hop - 1],
            recv_sem=pair_recv.at[hop - 1],
            device_id={"seq": lax.rem(me + 2 * hop, count)}, device_id_type=MESH,
        )

    for hop in range(1, groups):

        @pl.when(group + hop < groups)
        def _():
            pair_copy(hop).start()

    for h in range(half):
        row = jnp.where(place == 0, even_fade[h : h + 1], even_fade[half + h : half + h + 1])
        back[h] = jnp.broadcast_to(row, back.shape[1:])

    for copy in total_copies:
        copy.wait()
    span = jnp.zeros(total_ref.shape, F32)
    prior_ref[pl.ds(keep, half)] = jnp.zeros((half,) + prior_ref.shape[1:], F32)
    for hop in range(1, groups):

        @pl.when(group >= hop)
        def _():
            pair_copy(hop).wait_recv()
            factor = jnp.exp2(span)
            for h in range(half):
                row = jnp.where(place == 0, factor[h : h + 1], factor[half + h : half + h + 1])
                prior_ref[keep + h] += row * pairs[hop - 1, h].astype(F32)

        source = lax.rem(group - hop + groups, groups) * 2
        span += total_of(source) + total_of(source + 1)

    for hop in range(1, groups):

        @pl.when(group + hop < groups)
        def _():
            pair_copy(hop).wait_send()

    for h in range(half):
        before = prior_ref[keep + h]
        later = back[h] * before + start[h]
        sent[h] = (odd * before + (1.0 - odd) * later).astype(BF16)
        prior_ref[keep + h] = odd * later + (1.0 - odd) * before
    answer = pltpu.make_async_remote_copy(
        src_ref=sent, dst_ref=landed, send_sem=back_sems.at[0], recv_sem=back_sems.at[1],
        device_id={"seq": partner}, device_id_type=MESH,
    )
    answer.start()
    answer.wait()
    prior_ref[pl.ds(give, half)] = landed[...].astype(F32)


def comm_params(number):
    return pltpu.CompilerParams(
        collective_id=number, has_side_effects=True, vmem_limit_bytes=VMEM_BYTES
    )


def carried_state(seq, end_state, totals, number):
    heads, size, width = end_state.shape
    half = heads // 2
    groups = seq // 2
    dma = pltpu.SemaphoreType.DMA
    whole = pl.BlockSpec(memory_space=pltpu.VMEM)
    return pl.pallas_call(
        functools.partial(prior_kernel, seq),
        out_shape=jax.ShapeDtypeStruct(end_state.shape, F32),
        in_specs=[whole, whole],
        out_specs=whole,
        scratch_shapes=[
            pltpu.VMEM((seq,) + totals.shape, F32),
            pltpu.VMEM((half, size, width), BF16),
            pltpu.VMEM((half, size, width), BF16),
            pltpu.VMEM((half, size, width), BF16),
            pltpu.VMEM((max(groups - 1, 1), half, size, width), BF16),
            pltpu.VMEM((half, size, width), F32),
            pltpu.VMEM((half, size, width), F32),
            pltpu.VMEM((half, size, width), BF16),
            pltpu.VMEM(totals.shape, F32),
            dma((2,)),
            dma((seq - 1,)),
            dma((seq - 1,)),
            dma((2,)),
            dma((max(groups - 1, 1),)),
            dma((max(groups - 1, 1),)),
            dma((2,)),
        ],
        compiler_params=comm_params(number),
        name=f"prior_{number}",
    )(end_state, totals)


def layer(
    seq, number, inputs, x_spec, gate, write_mat, read_mat, step_mat, decay_mat, skip, cols,
    out, out_spec, norm_of=None,
):
    heads = step_mat.shape[0]
    size = write_mat.shape[0]
    blocks = step_mat.shape[1] // BLOCK
    features = gate.shape[-1]
    width = features // heads
    wide = pl.BlockSpec((size, BLOCK), lambda b: (0, b))
    thin = pl.BlockSpec((heads, BLOCK), lambda b: (0, b))
    rows = pl.BlockSpec((1, BLOCK, features), lambda b: (b, 0, 0))
    params = pltpu.CompilerParams(vmem_limit_bytes=VMEM_BYTES)
    scale_of, extra, extra_specs = None, (), []
    shapes = [
        jax.ShapeDtypeStruct((heads, size, width), F32),
        jax.ShapeDtypeStruct((heads, LANES), F32),
    ]
    specs = [
        pl.BlockSpec((heads, size, width), lambda b: (0, 0, 0)),
        pl.BlockSpec((heads, LANES), lambda b: (0, 0)),
    ]
    if norm_of is not None:
        scale_of, extra, extra_specs = norm_of
        shapes.append(jax.ShapeDtypeStruct((blocks, BLOCK, features), BF16))
        specs.append(rows)
    made = pl.pallas_call(
        functools.partial(states_kernel, heads, scale_of),
        grid=(blocks,),
        out_shape=shapes,
        in_specs=[*extra_specs, x_spec, wide, thin, thin],
        out_specs=specs,
        compiler_params=params,
        name=f"states_{number}",
    )(*extra, inputs, write_mat, step_mat, decay_mat)
    prior = carried_state(seq, made[0], made[1], number)
    if norm_of is not None:
        inputs, x_spec = made[2], rows
    depth = -(-blocks // 8) * 8
    return pl.pallas_call(
        functools.partial(main_kernel, heads, cols),
        grid=(blocks,),
        out_shape=(out, jax.ShapeDtypeStruct((depth, BLOCK), F32)),
        in_specs=[
            pl.BlockSpec(memory_space=pltpu.SMEM),
            x_spec,
            rows,
            wide,
            wide,
            thin,
            thin,
            pl.BlockSpec((heads, size, width), lambda b: (0, 0, 0)),
        ],
        out_specs=(out_spec, pl.BlockSpec((depth, BLOCK), lambda b: (0, 0))),
        scratch_shapes=[
            pltpu.VMEM((heads, size, width), F32), pltpu.VMEM((2, BLOCK, width), F32)
        ],
        compiler_params=params,
        name=f"main_{number}",
    )(skip, inputs, gate, write_mat, read_mat, step_mat, decay_mat, prior)


def body(
    seq, head, tokens_in, gate_rows, gate_cols, write_rows, read_rows, step_rows, decay_rows,
    skip_rows, norm_rows, write_cols, read_cols, step_cols, decay_cols, skip_cols, norm_cols,
):
    grid_rows, grid_cols, features = tokens_in.shape
    blocks = grid_rows * grid_cols // BLOCK
    high = BLOCK // grid_cols
    local_cols = grid_cols // seq
    all_rows = grid_rows * seq
    per_col = all_rows // BLOCK
    slabs = BLOCK // grid_rows
    inner = features * head
    dma = pltpu.SemaphoreType.DMA
    anywhere = pl.BlockSpec(memory_space=pl.ANY)
    whole = pl.BlockSpec(memory_space=pltpu.VMEM)
    rows = pl.BlockSpec((1, BLOCK, features), lambda b: (b, 0, 0))

    gated, squares = layer(
        seq, 0, tokens_in.reshape(blocks, BLOCK, features), rows,
        gate_rows.reshape(blocks, BLOCK, features),
        write_rows, read_rows, step_rows, decay_rows, skip_rows, grid_cols,
        jax.ShapeDtypeStruct((seq, local_cols, grid_rows, features), BF16),
        pl.BlockSpec((seq, local_cols, high, features), lambda b: (0, 0, b, 0)),
    )
    depth = squares.shape[0]
    hidden, scales = pl.pallas_call(
        functools.partial(trade_kernel, seq, head, inner),
        out_shape=(
            jax.ShapeDtypeStruct(gated.shape, BF16),
            jax.ShapeDtypeStruct((seq * depth, BLOCK), F32),
        ),
        in_specs=[anywhere, whole],
        out_specs=(anywhere, whole),
        scratch_shapes=[
            pltpu.VMEM((head - 1,) + squares.shape, F32),
            pltpu.VMEM(squares.shape, F32),
            dma((head - 1,)), dma((head - 1,)),
            dma((seq - 1,)), dma((seq - 1,)),
            dma((seq - 1,)), dma((seq - 1,)), dma(()),
        ],
        compiler_params=comm_params(2),
        name="trade",
    )(gated, squares)
    gate = jnp.transpose(gate_cols, (1, 0, 2)).reshape(local_cols * per_col, BLOCK, features)
    gated, squares = layer(
        seq, 1, hidden,
        pl.BlockSpec(
            (slabs, 1, grid_rows, features), lambda b: (b % per_col, b // per_col, 0, 0)
        ),
        gate, write_cols, read_cols, step_cols, decay_cols, skip_cols, 1,
        jax.ShapeDtypeStruct((local_cols * per_col, BLOCK, features), F32), rows,
        (
            functools.partial(column_scale, local_cols, per_col, grid_rows, grid_cols),
            (lax.axis_index("seq").reshape(1), scales, norm_rows.reshape(1, features)),
            [
                pl.BlockSpec(memory_space=pltpu.SMEM),
                pl.BlockSpec((slabs * depth, BLOCK), lambda b: (b % per_col, 0)),
                pl.BlockSpec((1, features), lambda b: (0, 0)),
            ],
        ),
    )
    squares = pl.pallas_call(
        functools.partial(sum_kernel, head),
        out_shape=jax.ShapeDtypeStruct(squares.shape, F32),
        in_specs=[whole],
        out_specs=whole,
        scratch_shapes=[
            pltpu.VMEM((head - 1,) + squares.shape, F32), dma((head - 1,)), dma((head - 1,)),
        ],
        compiler_params=comm_params(3),
        name="squares",
    )(squares)
    part = BLOCK // local_cols
    out_shape, out_spec = (all_rows, local_cols, features), (part, local_cols, features)
    if local_cols == 1:
        out_shape, out_spec = (all_rows, features), (part, features)
    result = pl.pallas_call(
        functools.partial(norm_kernel, inner, per_col),
        grid=(all_rows // part,),
        out_shape=jax.ShapeDtypeStruct(out_shape, BF16),
        in_specs=[
            pl.BlockSpec((local_cols, part, features), lambda q: (0, q, 0)),
            pl.BlockSpec(squares.shape, lambda q: (0, 0)),
            pl.BlockSpec((1, features), lambda q: (0, 0)),
        ],
        out_specs=pl.BlockSpec(out_spec, lambda q: (q,) + (0,) * (len(out_spec) - 1)),
        scratch_shapes=[pltpu.VMEM((2, BLOCK, LANES), F32)],
        compiler_params=pltpu.CompilerParams(vmem_limit_bytes=VMEM_BYTES),
        name="norm",
    )(gated.reshape(local_cols, all_rows, features), squares, norm_cols.reshape(1, features))
    return result.reshape(all_rows, local_cols, features)


def solution(mesh):
    placed = (
        P("seq", None, "head"),
        P("seq", None, "head"),
        P(None, "seq", "head"),
        P(None, "seq"),
        P(None, "seq"),
        P("head", "seq"),
        P("head", "seq"),
        P("head"),
        P("head"),
        P(None, "seq"),
        P(None, "seq"),
        P("head", "seq"),
        P("head", "seq"),
        P("head"),
        P("head"),
    )
    return jax.shard_map(
        functools.partial(body, mesh.shape["seq"], mesh.shape["head"]),
        mesh=mesh, in_specs=placed, out_specs=P(None, "seq", "head"), check_vma=False,
    )
```

```python
import functools
import jax
import jax.numpy as jnp
from jax import lax
from jax.experimental import pallas as pl
from jax.experimental.pallas import tpu as pltpu
from jax.sharding import PartitionSpec as P

BLOCK = 256
LANES = 128
EPSILON = 1e-05
LOG2E = 1.4426950408889634
HIGHEST = lax.Precision.HIGHEST
MESH = pl.DeviceIdType.MESH
F32 = jnp.float32
BF16 = jnp.bfloat16
VMEM_BYTES = 60 * 1024 * 1024


def contract(a, b, dims, precision=None):
    return lax.dot_general(
        a, b, (dims, ((), ())), precision=precision, preferred_element_type=F32
    )


def iota(shape, axis):
    return lax.broadcasted_iota(jnp.int32, shape, axis)


def block_sums(decay):
    upper = (iota((BLOCK, BLOCK), 0) <= iota((BLOCK, BLOCK), 1)).astype(F32)
    cumulative = contract(decay, upper, ((1,), (0,)), HIGHEST)
    total = contract(decay, jnp.ones((BLOCK, LANES), F32), ((1,), (0,)), HIGHEST)
    return cumulative, total


def head_state(write32, weight_row, tokens):
    loaded = (write32 * weight_row).astype(BF16)
    return contract(loaded, tokens, ((1,), (0,)))


def column_scale(local_cols, per_col, grid_rows, grid_cols, place_ref, scales):
    high = BLOCK // grid_cols
    column = place_ref[0] * local_cols + pl.program_id(0) // per_col
    shape = (BLOCK, scales.shape[0])
    row = iota(shape, 0)
    depth = scales.shape[0] * grid_rows // BLOCK
    source = (row // grid_rows) * depth + (row % grid_rows) // high
    picked = contract((iota(shape, 1) == source).astype(F32), scales, ((1,), (0,)), HIGHEST)
    lane = (iota((BLOCK, BLOCK), 0) % high) * grid_cols + column
    return jnp.sum(jnp.where(iota((BLOCK, BLOCK), 1) == lane, picked, 0.0), axis=1, keepdims=True)


def states_kernel(heads, scale_of, *refs):
    if scale_of is None:
        x_ref, write_ref, step_ref, decay_ref, end_ref, total_ref = refs
    else:
        (place_ref, scales_ref, gain_ref, x_ref, write_ref, step_ref, decay_ref, end_ref,
         total_ref, hidden_ref) = refs
    step_at = pl.program_id(0)

    @pl.when(step_at == 0)
    def _():
        end_ref[...] = jnp.zeros_like(end_ref)
        total_ref[...] = jnp.zeros_like(total_ref)

    cumulative, total = block_sums(decay_ref[...] * LOG2E)
    tokens = x_ref[...].reshape(BLOCK, x_ref.shape[-1])
    if scale_of is not None:
        scale = scale_of(place_ref, scales_ref[...])
    write32 = write_ref[...].astype(F32)
    final = total[:, :1]
    weights = jnp.exp2(final - cumulative) * step_ref[...]
    fade = jnp.exp2(total)
    for h in range(heads):
        lanes = slice(h * LANES, (h + 1) * LANES)
        own = tokens[:, lanes]
        if scale_of is not None:
            own = (own.astype(F32) * scale * gain_ref[:, lanes]).astype(BF16)
            hidden_ref[0, :, lanes] = own
        gained = head_state(write32, weights[h : h + 1], own)
        end_ref[h] = fade[h : h + 1] * end_ref[h] + gained
    total_ref[...] += total


def main_kernel(
    heads, cols, skip_ref, x_ref, gate_ref, write_ref, read_ref, step_ref, decay_ref, prior_ref,
    gated_ref, squares_ref, state, turned,
):
    @pl.when(pl.program_id(0) == 0)
    def _():
        state[...] = prior_ref[...]
        squares_ref[...] = jnp.zeros_like(squares_ref)

    main_block(
        heads, cols, pl.program_id(0), skip_ref, x_ref, gate_ref, write_ref, read_ref, step_ref,
        decay_ref, gated_ref, squares_ref, state, turned,
    )


def main_block(
    heads, cols, at, skip_ref, x_ref, gate_ref, write_ref, read_ref, step_ref, decay_ref,
    gated_ref, squares_ref, state, turned,
):
    decay = decay_ref[...] * LOG2E
    step = step_ref[...]
    cumulative, total = block_sums(decay)
    lower = (iota((BLOCK, BLOCK), 0) >= iota((BLOCK, BLOCK), 1)).astype(F32)
    across = contract(lower, decay, ((1,), (1,)), HIGHEST)
    lifting = jnp.exp2(across)
    tokens = x_ref[...].reshape(BLOCK, x_ref.shape[-1])
    write = write_ref[...]
    read = read_ref[...]
    write32 = write.astype(F32)
    scores = contract(read, write, ((0,), (0,))) * lower
    weights = jnp.exp2(total[:, :1] - cumulative) * step
    fade = jnp.exp2(total)
    squares = jnp.zeros((BLOCK, LANES), F32)
    read_twice = jnp.concatenate([read, read], axis=0)
    high = BLOCK // cols
    for h in range(heads):
        lanes = slice(h * LANES, (h + 1) * LANES)
        own = tokens[:, lanes]
        spread = jnp.minimum(across[:, h : h + 1] - cumulative[h : h + 1], 0.0)
        mixing = (jnp.exp2(spread) * scores * step[h : h + 1]).astype(BF16)
        held = state[h]
        loaded = (write32 * weights[h : h + 1]).astype(BF16)
        both = contract(jnp.concatenate([mixing, loaded], axis=0), own, ((1,), (0,)))
        out = both[:BLOCK]
        if h % 2 == 0:
            pair = jnp.concatenate([held] + ([state[h + 1]] if h + 1 < heads else []), axis=1)
            coarse = pair.astype(BF16)
            fine = (pair - coarse.astype(F32)).astype(BF16)
            parts = jnp.concatenate([coarse, fine], axis=0)
            from_state = contract(read_twice, parts, ((0,), (0,)))
        side = (h % 2) * LANES
        out += lifting[:, h : h + 1] * from_state[:, side : side + LANES]
        out += skip_ref[h] * own.astype(F32)
        gate = gate_ref[0, :, lanes].astype(F32)
        gated = out * (gate / (1.0 + jnp.exp2(gate * -LOG2E)))
        squares += gated * gated
        if cols > 1:
            near = gated_ref.shape[1]
            slot = turned.at[h % 2]
            slot[...] = gated
            for c in range(cols):
                gated_ref[c // near, c % near, :, lanes] = slot[
                    pl.ds(c, high, stride=cols), :
                ].astype(BF16)
        else:
            gated_ref[0, :, lanes] = gated
        state[h] = fade[h : h + 1] * held + both[BLOCK:]
    row = contract(jnp.ones((8, LANES), F32), squares, ((1,), (1,)), HIGHEST)
    squares_ref[pl.ds(at, 1), :] = row[:1]


def norm_kernel(inner, per_col, gated_ref, squares_ref, gain_ref, out_ref, turned):
    cols, rows, features = gated_ref.shape
    square = (BLOCK, BLOCK)
    start = pl.program_id(0) * rows
    lane = start % BLOCK + iota(square, 0) % rows
    sums = contract((lane == iota(square, 1)).astype(F32), squares_ref[...], ((1,), (1,)), HIGHEST)
    block = (iota(sums.shape, 0) // rows) * per_col + start // BLOCK
    sums = jnp.sum(jnp.where(iota(sums.shape, 1) == block, sums, 0.0), axis=1, keepdims=True)
    scaled = lax.rsqrt(sums / inner + EPSILON)
    for at in range(0, features, LANES):
        lanes = slice(at, at + LANES)
        result = gated_ref[:, :, lanes].reshape(BLOCK, LANES) * scaled * gain_ref[:, lanes]
        if cols > 1:
            slot = turned.at[at // LANES % 2]
            for c in range(cols):
                slot[pl.ds(c, rows, stride=cols), :] = result[c * rows : (c + 1) * rows]
            out_ref[:, :, lanes] = slot[...].reshape(rows, cols, LANES).astype(BF16)
        else:
            out_ref[:, lanes] = result.astype(BF16)


def greet(axes):
    greet_signal(axes)
    greet_wait(axes)


def greet_signal(axes):
    barrier = pltpu.get_barrier_semaphore()
    for axis, count in axes:
        me = lax.axis_index(axis)
        for hop in range(1, count):
            pl.semaphore_signal(
                barrier, inc=1, device_id={axis: lax.rem(me + hop, count)}, device_id_type=MESH
            )


def greet_wait(axes):
    pl.semaphore_wait(
        pltpu.get_barrier_semaphore(), sum(count - 1 for _, count in axes)
    )


def head_sum(count, own_ref, held, send_sems, recv_sems):
    me = lax.axis_index("head")
    copies = []
    for hop in range(1, count):
        copy = pltpu.make_async_remote_copy(
            src_ref=own_ref,
            dst_ref=held.at[hop - 1],
            send_sem=send_sems.at[hop - 1],
            recv_sem=recv_sems.at[hop - 1],
            device_id={"head": lax.rem(me + hop, count)},
            device_id_type=MESH,
        )
        copy.start()
        copies.append(copy)
    for copy in copies:
        copy.wait()
    total = own_ref[...]
    for hop in range(1, count):
        total += held[hop - 1]
    return total


def sum_kernel(count, own_ref, out_ref, held, send_sems, recv_sems):
    greet((("head", count),))
    out_ref[...] = head_sum(count, own_ref, held, send_sems, recv_sems)


def trade_kernel(
    count, head_count, inner, heads, cols, skip_ref, x_hbm, gate_hbm, write_ref, read_ref,
    step_ref, decay_ref, prior_ref, out_ref, scales_ref, x_ref, gate_ref, gated, squares, state,
    turned, held, scale, load_sems, sum_send, sum_recv, scale_send, scale_recv, send_sems,
    recv_sems, local_sems,
):
    axes = (("seq", count), ("head", head_count))
    blocks, features = x_ref.shape[0], x_ref.shape[-1]
    high = gated.shape[3]
    me = lax.axis_index("seq")
    greet_signal(axes)

    def load(b):
        return (
            pltpu.make_async_copy(x_hbm.at[b], x_ref.at[b], load_sems.at[0, b]),
            pltpu.make_async_copy(gate_hbm.at[b], gate_ref.at[b], load_sems.at[1, b]),
        )

    for b in range(blocks):
        for copy in load(b):
            copy.start()
    state[...] = prior_ref[...]
    squares[...] = jnp.zeros_like(squares)

    def compute(b):
        for copy in load(b):
            copy.wait()
        span = pl.ds(pl.multiple_of(b * BLOCK, BLOCK), BLOCK)
        one = pl.ds(b, 1)
        main_block(
            heads, cols, b, skip_ref, x_ref.at[one], gate_ref.at[one], write_ref.at[:, span],
            read_ref.at[:, span], step_ref.at[:, span], decay_ref.at[:, span], gated.at[b],
            squares, state, turned,
        )

    def rows_of(b):
        return out_ref.at[me, :, pl.ds(pl.multiple_of(b * high, high), high)]

    def send(b, ahead):
        to = lax.rem(me + ahead, count)
        return pltpu.make_async_remote_copy(
            src_ref=gated.at[b, to],
            dst_ref=rows_of(b),
            send_sem=send_sems.at[ahead - 1, b],
            recv_sem=recv_sems.at[ahead - 1, b],
            device_id={"seq": to},
            device_id_type=MESH,
        )

    def keep(b):
        return pltpu.make_async_copy(gated.at[b, me], rows_of(b), local_sems.at[b])

    def send_all(b):
        for hop in range(count // 2, count // 2 + count - 1):
            send(b, 1 + (hop - 1) % (count - 1)).start()
        keep(b).start()

    compute(0)
    greet_wait(axes)
    send_all(0)

    def step(b, carry):
        compute(b)
        send_all(b)
        return carry

    lax.fori_loop(1, blocks, step, 0)
    total = head_sum(head_count, squares, held, sum_send, sum_recv)
    scale[...] = lax.rsqrt(total / inner + EPSILON)
    depth = scale.shape[0]
    mine = pl.ds(pl.multiple_of(me * depth, depth), depth)
    copies = []
    for hop in range(1, count):
        copy = pltpu.make_async_remote_copy(
            src_ref=scale,
            dst_ref=scales_ref.at[mine],
            send_sem=scale_send.at[hop - 1],
            recv_sem=scale_recv.at[hop - 1],
            device_id={"seq": lax.rem(me + hop, count)},
            device_id_type=MESH,
        )
        copy.start()
        copies.append(copy)
    scales_ref[mine, :] = scale[...]
    for copy in copies:
        copy.wait()

    def settle(b, carry):
        keep(b).wait()
        for ahead in range(1, count):
            send(b, ahead).wait()
        return carry

    lax.fori_loop(0, blocks, settle, 0)


def prior_kernel(
    count, end_ref, total_ref, prior_ref, totals, sent, swapped, pair, pairs, back, start, landed, near,
    near_sems, total_send, total_recv, swap_sems, pair_send, pair_recv, back_sems,
):
    heads = end_ref.shape[0]
    half = heads // 2
    greet((("seq", count),))
    me = lax.axis_index("seq")
    place = lax.rem(me, 2)
    partner = me + 1 - 2 * place
    group = me // 2
    groups = count // 2
    keep = place * half
    give = half - keep

    sent[...] = end_ref[pl.ds(give, half)].astype(BF16)
    swap = pltpu.make_async_remote_copy(
        src_ref=sent, dst_ref=swapped, send_sem=swap_sems.at[0], recv_sem=swap_sems.at[1],
        device_id={"seq": partner}, device_id_type=MESH,
    )
    swap.start()
    near_copy = pltpu.make_async_remote_copy(
        src_ref=total_ref, dst_ref=near, send_sem=near_sems.at[0], recv_sem=near_sems.at[1],
        device_id={"seq": partner}, device_id_type=MESH,
    )
    near_copy.start()
    total_copies = []
    for hop in range(1, count):
        copy = pltpu.make_async_remote_copy(
            src_ref=total_ref, dst_ref=totals.at[hop], send_sem=total_send.at[hop - 1],
            recv_sem=total_recv.at[hop - 1],
            device_id={"seq": lax.rem(me + hop, count)}, device_id_type=MESH,
        )
        copy.start()
        total_copies.append(copy)
    totals[0] = total_ref[...]
    near_copy.wait()
    swap.wait()

    def total_of(device):
        return totals[lax.rem(me - device + count, count)]

    odd = place.astype(F32)
    odd_fade = jnp.exp2(jnp.where(place == 0, near[...], total_ref[...]))
    even_fade = jnp.exp2(jnp.where(place == 0, total_ref[...], near[...]))
    for h in range(half):
        mine = end_ref[keep + h]
        other = swapped[h].astype(F32)
        first = odd * other + (1.0 - odd) * mine
        last = odd * mine + (1.0 - odd) * other
        row = jnp.where(place == 0, odd_fade[h : h + 1], odd_fade[half + h : half + h + 1])
        pair[h] = (row * first + last).astype(BF16)
        start[h] = first

    def pair_copy(hop):
        return pltpu.make_async_remote_copy(
            src_ref=pair, dst_ref=pairs.at[hop - 1], send_sem=pair_send.at[hop - 1],
            recv_sem=pair_recv.at[hop - 1],
            device_id={"seq": lax.rem(me + 2 * hop, count)}, device_id_type=MESH,
        )

    for hop in range(1, groups):

        @pl.when(group + hop < groups)
        def _():
            pair_copy(hop).start()

    for h in range(half):
        row = jnp.where(place == 0, even_fade[h : h + 1], even_fade[half + h : half + h + 1])
        back[h] = jnp.broadcast_to(row, back.shape[1:])

    for copy in total_copies:
        copy.wait()
    span = jnp.zeros(total_ref.shape, F32)
    prior_ref[pl.ds(keep, half)] = jnp.zeros((half,) + prior_ref.shape[1:], F32)
    for hop in range(1, groups):

        @pl.when(group >= hop)
        def _():
            pair_copy(hop).wait_recv()
            factor = jnp.exp2(span)
            for h in range(half):
                row = jnp.where(place == 0, factor[h : h + 1], factor[half + h : half + h + 1])
                prior_ref[keep + h] += row * pairs[hop - 1, h].astype(F32)

        source = lax.rem(group - hop + groups, groups) * 2
        span += total_of(source) + total_of(source + 1)

    for hop in range(1, groups):

        @pl.when(group + hop < groups)
        def _():
            pair_copy(hop).wait_send()

    for h in range(half):
        before = prior_ref[keep + h]
        later = back[h] * before + start[h]
        sent[h] = (odd * before + (1.0 - odd) * later).astype(BF16)
        prior_ref[keep + h] = odd * later + (1.0 - odd) * before
    answer = pltpu.make_async_remote_copy(
        src_ref=sent, dst_ref=landed, send_sem=back_sems.at[0], recv_sem=back_sems.at[1],
        device_id={"seq": partner}, device_id_type=MESH,
    )
    answer.start()
    answer.wait()
    prior_ref[pl.ds(give, half)] = landed[...].astype(F32)


def comm_params(number):
    return pltpu.CompilerParams(
        collective_id=number, has_side_effects=True, vmem_limit_bytes=VMEM_BYTES
    )


def carried_state(seq, end_state, totals, number):
    heads, size, width = end_state.shape
    half = heads // 2
    groups = seq // 2
    dma = pltpu.SemaphoreType.DMA
    whole = pl.BlockSpec(memory_space=pltpu.VMEM)
    return pl.pallas_call(
        functools.partial(prior_kernel, seq),
        out_shape=jax.ShapeDtypeStruct(end_state.shape, F32),
        in_specs=[whole, whole],
        out_specs=whole,
        scratch_shapes=[
            pltpu.VMEM((seq,) + totals.shape, F32),
            pltpu.VMEM((half, size, width), BF16),
            pltpu.VMEM((half, size, width), BF16),
            pltpu.VMEM((half, size, width), BF16),
            pltpu.VMEM((max(groups - 1, 1), half, size, width), BF16),
            pltpu.VMEM((half, size, width), F32),
            pltpu.VMEM((half, size, width), F32),
            pltpu.VMEM((half, size, width), BF16),
            pltpu.VMEM(totals.shape, F32),
            dma((2,)),
            dma((seq - 1,)),
            dma((seq - 1,)),
            dma((2,)),
            dma((max(groups - 1, 1),)),
            dma((max(groups - 1, 1),)),
            dma((2,)),
        ],
        compiler_params=comm_params(number),
        name=f"prior_{number}",
    )(end_state, totals)


def layer(
    seq, number, inputs, x_spec, gate, write_mat, read_mat, step_mat, decay_mat, skip, cols,
    out, out_spec, norm_of=None, send=None,
):
    heads = step_mat.shape[0]
    size = write_mat.shape[0]
    blocks = step_mat.shape[1] // BLOCK
    features = gate.shape[-1]
    width = features // heads
    wide = pl.BlockSpec((size, BLOCK), lambda b: (0, b))
    thin = pl.BlockSpec((heads, BLOCK), lambda b: (0, b))
    rows = pl.BlockSpec((1, BLOCK, features), lambda b: (b, 0, 0))
    params = pltpu.CompilerParams(vmem_limit_bytes=VMEM_BYTES)
    scale_of, extra, extra_specs = None, (), []
    shapes = [
        jax.ShapeDtypeStruct((heads, size, width), F32),
        jax.ShapeDtypeStruct((heads, LANES), F32),
    ]
    specs = [
        pl.BlockSpec((heads, size, width), lambda b: (0, 0, 0)),
        pl.BlockSpec((heads, LANES), lambda b: (0, 0)),
    ]
    if norm_of is not None:
        scale_of, extra, extra_specs = norm_of
        shapes.append(jax.ShapeDtypeStruct((blocks, BLOCK, features), BF16))
        specs.append(rows)
    made = pl.pallas_call(
        functools.partial(states_kernel, heads, scale_of),
        grid=(blocks,),
        out_shape=shapes,
        in_specs=[*extra_specs, x_spec, wide, thin, thin],
        out_specs=specs,
        compiler_params=params,
        name=f"states_{number}",
    )(*extra, inputs, write_mat, step_mat, decay_mat)
    prior = carried_state(seq, made[0], made[1], number)
    if norm_of is not None:
        inputs, x_spec = made[2], rows
    depth = -(-blocks // 8) * 8
    if send is not None:
        return send(skip, inputs, gate, write_mat, read_mat, step_mat, decay_mat, prior)
    return pl.pallas_call(
        functools.partial(main_kernel, heads, cols),
        grid=(blocks,),
        out_shape=(out, jax.ShapeDtypeStruct((depth, BLOCK), F32)),
        in_specs=[
            pl.BlockSpec(memory_space=pltpu.SMEM),
            x_spec,
            rows,
            wide,
            wide,
            thin,
            thin,
            pl.BlockSpec((heads, size, width), lambda b: (0, 0, 0)),
        ],
        out_specs=(out_spec, pl.BlockSpec((depth, BLOCK), lambda b: (0, 0))),
        scratch_shapes=[
            pltpu.VMEM((heads, size, width), F32), pltpu.VMEM((2, BLOCK, width), F32)
        ],
        compiler_params=params,
        name=f"main_{number}",
    )(skip, inputs, gate, write_mat, read_mat, step_mat, decay_mat, prior)


def body(
    seq, head, tokens_in, gate_rows, gate_cols, write_rows, read_rows, step_rows, decay_rows,
    skip_rows, norm_rows, write_cols, read_cols, step_cols, decay_cols, skip_cols, norm_cols,
):
    grid_rows, grid_cols, features = tokens_in.shape
    blocks = grid_rows * grid_cols // BLOCK
    high = BLOCK // grid_cols
    local_cols = grid_cols // seq
    all_rows = grid_rows * seq
    per_col = all_rows // BLOCK
    slabs = BLOCK // grid_rows
    inner = features * head
    dma = pltpu.SemaphoreType.DMA
    anywhere = pl.BlockSpec(memory_space=pl.ANY)
    whole = pl.BlockSpec(memory_space=pltpu.VMEM)
    rows = pl.BlockSpec((1, BLOCK, features), lambda b: (b, 0, 0))

    heads, size = step_rows.shape[0], write_rows.shape[0]
    width = features // heads
    depth = -(-blocks // 8) * 8
    send = pl.pallas_call(
        functools.partial(trade_kernel, seq, head, inner, heads, grid_cols),
        out_shape=(
            jax.ShapeDtypeStruct((seq, local_cols, grid_rows, features), BF16),
            jax.ShapeDtypeStruct((seq * depth, BLOCK), F32),
        ),
        in_specs=[pl.BlockSpec(memory_space=pltpu.SMEM), anywhere, anywhere] + [whole] * 5,
        out_specs=(anywhere, whole),
        scratch_shapes=[
            pltpu.VMEM((blocks, BLOCK, features), BF16),
            pltpu.VMEM((blocks, BLOCK, features), BF16),
            pltpu.VMEM((blocks, seq, local_cols, high, features), BF16),
            pltpu.VMEM((depth, BLOCK), F32),
            pltpu.VMEM((heads, size, width), F32),
            pltpu.VMEM((2, BLOCK, width), F32),
            pltpu.VMEM((head - 1, depth, BLOCK), F32),
            pltpu.VMEM((depth, BLOCK), F32),
            dma((2, blocks)),
            dma((head - 1,)), dma((head - 1,)),
            dma((seq - 1,)), dma((seq - 1,)),
            dma((seq - 1, blocks)), dma((seq - 1, blocks)), dma((blocks,)),
        ],
        compiler_params=comm_params(2),
        name="trade",
    )
    hidden, scales = layer(
        seq, 0, tokens_in.reshape(blocks, BLOCK, features), rows,
        gate_rows.reshape(blocks, BLOCK, features),
        write_rows, read_rows, step_rows, decay_rows, skip_rows, grid_cols, None, None, None, send,
    )
    gate = jnp.transpose(gate_cols, (1, 0, 2)).reshape(local_cols * per_col, BLOCK, features)
    gated, squares = layer(
        seq, 1, hidden,
        pl.BlockSpec(
            (slabs, 1, grid_rows, features), lambda b: (b % per_col, b // per_col, 0, 0)
        ),
        gate, write_cols, read_cols, step_cols, decay_cols, skip_cols, 1,
        jax.ShapeDtypeStruct((local_cols * per_col, BLOCK, features), F32), rows,
        (
            functools.partial(column_scale, local_cols, per_col, grid_rows, grid_cols),
            (lax.axis_index("seq").reshape(1), scales, norm_rows.reshape(1, features)),
            [
                pl.BlockSpec(memory_space=pltpu.SMEM),
                pl.BlockSpec((slabs * depth, BLOCK), lambda b: (b % per_col, 0)),
                pl.BlockSpec((1, features), lambda b: (0, 0)),
            ],
        ),
    )
    squares = pl.pallas_call(
        functools.partial(sum_kernel, head),
        out_shape=jax.ShapeDtypeStruct(squares.shape, F32),
        in_specs=[whole],
        out_specs=whole,
        scratch_shapes=[
            pltpu.VMEM((head - 1,) + squares.shape, F32), dma((head - 1,)), dma((head - 1,)),
        ],
        compiler_params=comm_params(3),
        name="squares",
    )(squares)
    part = BLOCK // local_cols
    out_shape, out_spec = (all_rows, local_cols, features), (part, local_cols, features)
    if local_cols == 1:
        out_shape, out_spec = (all_rows, features), (part, features)
    result = pl.pallas_call(
        functools.partial(norm_kernel, inner, per_col),
        grid=(all_rows // part,),
        out_shape=jax.ShapeDtypeStruct(out_shape, BF16),
        in_specs=[
            pl.BlockSpec((local_cols, part, features), lambda q: (0, q, 0)),
            pl.BlockSpec(squares.shape, lambda q: (0, 0)),
            pl.BlockSpec((1, features), lambda q: (0, 0)),
        ],
        out_specs=pl.BlockSpec(out_spec, lambda q: (q,) + (0,) * (len(out_spec) - 1)),
        scratch_shapes=[pltpu.VMEM((2, BLOCK, LANES), F32)],
        compiler_params=pltpu.CompilerParams(vmem_limit_bytes=VMEM_BYTES),
        name="norm",
    )(gated.reshape(local_cols, all_rows, features), squares, norm_cols.reshape(1, features))
    return result.reshape(all_rows, local_cols, features)


def solution(mesh):
    placed = (
        P("seq", None, "head"),
        P("seq", None, "head"),
        P(None, "seq", "head"),
        P(None, "seq"),
        P(None, "seq"),
        P("head", "seq"),
        P("head", "seq"),
        P("head"),
        P("head"),
        P(None, "seq"),
        P(None, "seq"),
        P("head", "seq"),
        P("head", "seq"),
        P("head"),
        P("head"),
    )
    return jax.shard_map(
        functools.partial(body, mesh.shape["seq"], mesh.shape["head"]),
        mesh=mesh, in_specs=placed, out_specs=P(None, "seq", "head"), check_vma=False,
    )
```
